512 devices in a mesh: mem: 32 (over x_hi, z), gx: 4 (over x_lo, core), gy: 4 (over y).
Axes of the slice: x: 4 (x_hi: 2, x_lo: 2; x = x_hi * 2 + x_lo), y: 4, z: 16, core: 2. Of those that a mesh axis runs over, the one named last changes fastest.
Arguments:
- control: float32 [64, 1024, 1024], P('mem', 'gx', 'gy'), may hold values from -6 to 6
- ensemble: bfloat16 [64, 1024, 1024], P('mem', 'gx', 'gy'), may hold values from -0.75 to 0.75
- obs_index: int32 [1024, 256], P('gx', 'gy'), may hold values from 0 to 255
- obs_value: float32 [1024, 256], P('gx', 'gy'), may hold values from -12 to 12
- obs_weight: float32 [1024, 256], P('gx', 'gy'), may hold values from 1 to 16
Outputs:
- gradient: float32 [64, 1024, 1024], P('mem', 'gx', 'gy')
The draws below stay inside these ranges and needn't reach their ends.
Inputs may be any that keep to these rules, and one draw needn't show every extreme that they name: obs_index[r, j] is a column inside the y tile j // 64; several observations may share a cell.
All inputs are finite; a program needn't handle non-finite values.
Results may differ from the reference program's by a relative error of at most 0.0003.
Values sent between devices are 32-bit elements; how exact they have to be, the bound alone decides.
A program may use at most 64 MiB of HBM per device.

```python
import math
import jax
import jax.numpy as jnp
from jax import lax

CY = 256
LEN = 400
MEMBERS = 64
NX = 1024
NY = 1024
OBS = 64
N_GY = 4


def draw_control(key, part):
    grid_shape = (MEMBERS, NX, NY)
    return jnp.clip(jax.random.normal(jax.random.fold_in(key, 17), grid_shape, jnp.float32), -6.0, 6.0)


def place_ends(array, key, least, high):
    extent = array.shape
    place = [jax.random.randint(jax.random.fold_in(key, axis), (), 0, extent[axis]) for axis in range(len(extent))]
    array = array.at[tuple(place)].set(least)
    longest = extent.index(max(extent))
    place[longest] = (place[longest] + 1) % extent[longest]
    return array.at[tuple(place)].set(high)


def shard_levels(rng, shape, pieces, smallest, high):
    factor_of = 1.0
    for position, blocks in pieces:
        heights = jax.random.uniform(jax.random.fold_in(jax.random.fold_in(rng, 6), position), (blocks,), jnp.float32, smallest / len(pieces), high / len(pieces))
        factor_of = factor_of * jnp.repeat(jnp.exp(heights), shape[position] // blocks).reshape((-1,) + (1,) * (len(shape) - 1 - position))
    return factor_of


def normal_values(key, extent, scale, reach, cuts=(), held_as=jnp.bfloat16):
    level = shard_levels(key, extent, cuts, -0.22, 0.18) if cuts else 1.0
    values = jax.random.normal(key, extent, jnp.float32) * scale * level
    return jnp.minimum(jnp.maximum(values, -reach), reach).astype(held_as)


def setup_inputs(seed: int = 0) -> dict:
    arg_keys = jax.random.split(jax.random.key(seed), 6)
    control = draw_control(jax.random.fold_in(arg_keys[5], 71), 0)
    ensemble = normal_values(arg_keys[1], (MEMBERS, NX, NY), 0.125, 0.75, ((0, 32), (1, 4), (2, 4)))
    obs_index = place_ends(jax.random.randint(arg_keys[2], (NX, N_GY * OBS), 0, CY), jax.random.fold_in(arg_keys[2], 1), 0, CY - 1).astype(jnp.int32)
    obs_value = normal_values(arg_keys[3], (NX, N_GY * OBS), 2.0, 12.0, ((0, 4), (1, 4)), jnp.float32)
    obs_weight = jnp.clip(jnp.exp(math.log(16.0) - 2.7725887 * jax.random.uniform(arg_keys[4], (NX, N_GY * OBS), jnp.float32) ** shard_levels(arg_keys[4], (NX, N_GY * OBS), ((0, 4), (1, 4)), -0.2, 0.2)), 1.0, 16.0)
    return dict(control=control, ensemble=ensemble, obs_index=obs_index, obs_value=obs_value, obs_weight=obs_weight)


saturation = 1.5

def pair_scale():
    decay_rate = math.exp(-1.0 / LEN)
    return (1.0 - decay_rate * decay_rate) / (1.0 + decay_rate * decay_rate)

def recurse(grid_field, backward):
    decay_rate = math.exp(-1.0 / LEN)
    unit_gain = math.sqrt(1.0 - decay_rate * decay_rate)

    def stepper(carried, sliced):
        updated = decay_rate * carried + unit_gain * sliced
        return (updated, updated)
    _, filtered = lax.scan(stepper, jnp.zeros_like(grid_field[0]), grid_field, reverse=backward)
    return filtered

def smooth(grid_field):
    along_x = recurse(recurse(grid_field, False), True)
    return pair_scale() * recurse(recurse(along_x.T, False), True).T

def smooth_adjoint(grid_field):
    along_y = recurse(recurse(grid_field.T, False), True).T
    return pair_scale() * recurse(recurse(along_y, False), True)

def obs_forcing(grid_field, columns, values, weights):
    picked = jnp.take_along_axis(grid_field, columns, axis=1)
    misfit = picked - values
    residual = weights * saturation * jnp.tanh(misfit / saturation)
    row_ids = lax.broadcasted_iota(jnp.int32, columns.shape, 0)
    return jnp.zeros_like(grid_field).at[row_ids, columns].add(residual)

def reference(control, ensemble, obs_index, obs_value, obs_weight):

    def add_member(running, member_pair):
        member_control, member_ens = member_pair
        return (running + member_ens * smooth(member_control), None)
    increment, _ = lax.scan(add_member, jnp.zeros_like(control[0]), (control, ensemble))
    tile_base = lax.broadcasted_iota(jnp.int32, obs_index.shape, 1) // OBS * CY
    columns = (obs_index + tile_base).astype(jnp.int32)
    forcing = obs_forcing(increment, columns, obs_value, obs_weight)

    def member_gradient(member_pair):
        member_control, member_ens = member_pair
        return member_control + smooth_adjoint(member_ens * forcing)
    return lax.map(member_gradient, (control, ensemble))
```

```python
import functools
import math

import jax
import jax.numpy as jnp
from jax import lax
from jax.experimental import pallas as pl
from jax.experimental.pallas import tpu as pltpu
from jax.sharding import PartitionSpec as P

LEN = 400
TILE = 256
GRID = 4
RING = 16
NX = GRID * TILE
OBS = 64
saturation = 1.5
MESH = pl.DeviceIdType.MESH
f32 = jnp.float32
bf16 = jnp.bfloat16
i32 = jnp.int32
FAR = 1 << 20

PLANE = [(dx, dy) for dy in (2, 1, 3, 0) for dx in (2, 3, 1, 0) if (dx, dy) != (0, 0)]
GATHER = [(dz, dx) for dz in (2, 1, -1, 0) for dx in (1, 0) if (dz, dx) != (0, 0)]
SPREAD = [(-dz, dx) for dz, dx in GATHER]
ACROSS = [(8, 0), (4, 0), (-4, 0)]


def pair_scale():
    decay_rate = math.exp(-1.0 / LEN)
    return (1.0 - decay_rate * decay_rate) / (1.0 + decay_rate * decay_rate)


def decay(steps):
    return jnp.exp(steps.astype(f32) * (-1.0 / LEN))


def split(x):
    high = x.astype(bf16)
    return high, (x - high.astype(f32)).astype(bf16)


def dot(a, b, left=1, right=0):
    return lax.dot_general(a, b, (((left,), (right,)), ((), ())), preferred_element_type=f32)


def take(x, lanes):
    return jnp.take_along_axis(x, lanes, axis=1)


def iota(shape, dim):
    return lax.broadcasted_iota(i32, shape, dim)


def in_plane(dx, dy):
    return {
        "gx": lax.rem(lax.axis_index("gx") + dx, GRID),
        "gy": lax.rem(lax.axis_index("gy") + dy, GRID),
    }


def in_mem(dz, dx):
    mem = lax.axis_index("mem")
    z, half = lax.rem(mem, RING), mem // RING
    return {"mem": lax.rem(half + dx, 2) * RING + lax.rem(z + dz + RING, RING)}


def piece_of(dz, dx):
    mem = lax.axis_index("mem")
    z, half = lax.rem(mem, RING), mem // RING
    return lax.rem(z + dz + RING, 4) * 2 + lax.rem(half + dx, 2)


def coefficients(axis, d, even, shape):
    me = lax.axis_index(axis)
    it = lax.rem(me - d + GRID, GRID)
    before = jnp.where(it < me, TILE * (me - it - 1) + 1, FAR)
    after = jnp.where(it > me, TILE * (it - me - 1) + 1, FAR)
    ends = 2 * NX - TILE * (me + it + 2) + 2
    own = decay(jnp.where(even, before, after))
    above = jnp.where(even, 0.0, -decay(jnp.full(shape, ends, i32)))
    return own, above


def kernel(
    control, ensemble, obs_index, obs_value, obs_weight, out,
    ctl, ens, idx, val, wgt, thi, tlo, vhi, vlo, w0, part, idxp, first,
    msg, rx, ry, rg, pkb, gat, mid, acr, resb,
    load_sem, plane_send, plane_recv, gs, gr, xs, xr, ss, sr,
):
    own = piece_of(0, 0)
    loads = [
        pltpu.make_async_copy(control, ctl, load_sem.at[0]),
        pltpu.make_async_copy(obs_index, idx, load_sem.at[1]),
        pltpu.make_async_copy(ensemble, ens, load_sem.at[2]),
    ]
    for half in range(2):
        rows = pl.ds(pl.multiple_of(half * 128 + own * 16, 16), 16)
        loads.append(pltpu.make_async_copy(obs_value.at[rows], val.at[half], load_sem.at[3 + half]))
        loads.append(pltpu.make_async_copy(obs_weight.at[rows], wgt.at[half], load_sem.at[5 + half]))
    for copy in loads:
        copy.start()

    barrier = pltpu.get_barrier_semaphore()
    peers = [in_plane(*o) for o in PLANE]
    peers += [in_mem(*o) for o in sorted(set(GATHER + SPREAD + ACROSS))]
    for peer in peers:
        pl.semaphore_signal(barrier, 1, device_id=peer, device_id_type=MESH)

    square = (TILE, TILE)
    table = decay(jnp.abs(iota(square, 0) - iota(square, 1)))
    high, low = split(table)
    thi[...] = high
    tlo[...] = low
    wide = (8, TILE)
    row, column = iota(wide, 0), iota(wide, 1)
    even = (row & 1) == 0
    ends = decay(jnp.where(even, TILE - 1 - column, column))
    starts = decay(jnp.where(even, column, TILE - 1 - column))
    f_row, b_row = ends[0:1], ends[1:2]
    ends_hi = ends.astype(bf16).astype(f32)
    ends16 = jnp.concatenate([ends_hi, ends - ends_hi], axis=0).astype(bf16)
    narrow = (8, 128)
    left = iota(narrow, 1) < 64
    cx = [coefficients("gx", d, even, wide) for d in range(GRID)]
    cy = [coefficients("gy", d, even, wide) for d in range(GRID)]
    cl = [coefficients("gy", d, left, narrow) for d in range(GRID)]
    lane16 = iota((16, 128), 1)
    left16 = lane16 < 64

    def fold(x):
        return x[0:8] + x[8:16]

    sends = []

    def begin(turn):
        sums = []
        for side in range(2):
            for m in range(2):
                sums.append(fold(dot(ends16, vhi[m], 1, side) + dot(ends16, vlo[m], 1, side)))
        x = jnp.where(row < 2, sums[0], jnp.where(row < 4, sums[1], jnp.where(row < 6, sums[2], sums[3])))
        x_hi = x.astype(bf16).astype(f32)
        x16 = jnp.concatenate([x_hi, x - x_hi], axis=0).astype(bf16)
        corner_f = jnp.sum(x * f_row, axis=1, keepdims=True)
        corner_b = jnp.sum(x * b_row, axis=1, keepdims=True)
        msg[turn, :, 0:TILE] = fold(dot(x16, thi[...]) + dot(x16, tlo[...]))
        msg[turn, :, TILE:] = jnp.where(left, corner_f, corner_b)
        copies = []
        for n, (dx, dy) in enumerate(PLANE):
            if dy == 0:
                src, dst = msg.at[turn], rx.at[turn, dx]
            elif dx == 0:
                src, dst = msg.at[turn], ry.at[turn, dy]
            else:
                src, dst = msg.at[turn, :, pl.ds(TILE, 128)], rg.at[turn, n]
            copy = pltpu.make_async_remote_copy(
                src, dst, plane_send.at[turn, n], plane_recv.at[turn, n],
                device_id=in_plane(dx, dy), device_id_type=MESH,
            )
            copy.start()
            copies.append(copy)
        sends.extend(copies)
        for m in range(2):
            u = dot(thi[...], vhi[m]) + dot(tlo[...], vhi[m]) + dot(thi[...], vlo[m])
            uhi, ulo = split(u)
            w0[m] = dot(uhi, thi[...]) + dot(ulo, thi[...]) + dot(uhi, tlo[...])
        return copies

    def finish(turn, copies):
        for copy in copies:
            copy.wait_recv()
        xs_, ys_ = 0.0, 0.0
        for d in range(GRID):
            a = msg[turn, :, 0:TILE] if d == 0 else rx[turn, d, :, 0:TILE]
            xs_ = xs_ + cx[d][0] * a + cx[d][1] * pltpu.roll(a, 1, 0)
            a = msg[turn, :, 0:TILE] if d == 0 else ry[turn, d, :, 0:TILE]
            ys_ = ys_ + cy[d][0] * a + cy[d][1] * pltpu.roll(a, 1, 0)
        corner = 0.0
        for dy in range(GRID):
            over_x = 0.0
            for dx in range(GRID):
                if (dx, dy) == (0, 0):
                    g = msg[turn, :, TILE:]
                elif dy == 0:
                    g = rx[turn, dx, :, TILE:]
                elif dx == 0:
                    g = ry[turn, dy, :, TILE:]
                else:
                    g = rg[turn, PLANE.index((dx, dy))]
                over_x = over_x + cx[dx][0][:, 0:128] * g + cx[dx][1][:, 0:128] * pltpu.roll(g, 1, 0)
            corner = corner + cl[dy][0] * over_x + cl[dy][1] * pltpu.roll(over_x, 64, 1)
        ab = jnp.where(row < 4, xs_ + corner[:, 0:1] * b_row + corner[:, 64:65] * f_row, ys_)
        a = jnp.where(row < 4, starts, ab)
        b = jnp.where(row < 4, ab, starts)
        b = jnp.concatenate([jnp.where((row & 2) == 0, b, 0.0), jnp.where((row & 2) == 0, 0.0, b)], axis=1)
        a_hi, b_hi = a.astype(bf16).astype(f32), b.astype(bf16).astype(f32)
        a_lo, b_lo = a - a_hi, b - b_hi
        a = jnp.concatenate([a_hi, a_hi, a_lo, a_lo], axis=0).astype(bf16)
        b = jnp.concatenate([b_hi, b_lo, b_hi, b_lo], axis=0).astype(bf16)
        return dot(a, b, 0, 0)

    loads[0].wait()
    for m in range(2):
        high, low = split(ctl[m])
        vhi[m] = high
        vlo[m] = low
    pl.semaphore_wait(barrier, len(peers))
    copies = begin(0)
    for copy in loads[1:]:
        copy.wait()
    idxp[...] = jnp.concatenate([idx[0:128], idx[128:256]], axis=1)
    update = finish(0, copies)
    part[...] = (
        ens[0].astype(f32) * (w0[0] + update[:, 0:TILE])
        + ens[1].astype(f32) * (w0[1] + update[:, TILE:])
    )

    def pick(k, carry):
        top = pl.ds(pl.multiple_of(k * 16, 16), 16)
        bottom = pl.ds(pl.multiple_of(128 + k * 16, 16), 16)
        at = idxp[top, :]
        low = at & 127
        upper = at >= 128
        above = jnp.where(upper, take(part[top, 128:256], low), take(part[top, 0:128], low))
        below = jnp.where(upper, take(part[bottom, 128:256], low), take(part[bottom, 0:128], low))
        pkb[k] = jnp.where(left16, above, below)
        return carry

    lax.fori_loop(0, 8, pick, 0)

    copies = []
    for n, (dz, dx) in enumerate(GATHER):
        copy = pltpu.make_async_remote_copy(
            pkb.at[piece_of(dz, dx)], gat.at[n], gs.at[n], gr.at[n],
            device_id=in_mem(dz, dx), device_id_type=MESH,
        )
        copy.start()
        copies.append(copy)
    sends.extend(copies)

    at = idxp[pl.ds(pl.multiple_of(own * 16, 16), 16), :]
    link = jnp.full((16, 128), -1, i32)
    for j in range(OBS):
        here = jnp.where(left16, at[:, j : j + 1], at[:, OBS + j : OBS + j + 1])
        where_ = jnp.where(left16, j, OBS + j)
        link = jnp.where((here == at) & (lane16 > where_), where_, link)
    links = []
    for level in range(6):
        links.append(link)
        link = jnp.where(link >= 0, take(link, jnp.maximum(link, 0)), -1)
    value = jnp.concatenate([val[0], val[1]], axis=1)
    weight = jnp.concatenate([wgt[0], wgt[1]], axis=1) * (saturation * pair_scale())

    total = pkb[own]
    for n, copy in enumerate(copies):
        copy.wait_recv()
        total = total + gat[n]
    mid[...] = total
    copies = []
    for n, (dz, dx) in enumerate(ACROSS):
        copy = pltpu.make_async_remote_copy(
            mid, acr.at[n], xs.at[n], xr.at[n], device_id=in_mem(dz, dx), device_id_type=MESH
        )
        copy.start()
        copies.append(copy)
    sends.extend(copies)

    def find(k, carry):
        at = idxp[pl.ds(pl.multiple_of(k * 8, 8), 8), :]
        lane = iota(narrow, 1)
        found = [jnp.full(narrow, -1, i32) for _ in range(4)]
        for j in range(OBS):
            for half in range(2):
                here = jnp.broadcast_to(at[:, half * OBS + j : half * OBS + j + 1], narrow)
                found[half * 2] = jnp.where(here == lane, half * OBS + j, found[half * 2])
                found[half * 2 + 1] = jnp.where(here == lane + 128, half * OBS + j, found[half * 2 + 1])
        for half in range(2):
            rows = pl.ds(pl.multiple_of(half * 128 + k * 8, 8), 8)
            first[rows, 0:128] = found[half * 2]
            first[rows, 128:256] = found[half * 2 + 1]
        return carry

    lax.fori_loop(0, 16, find, 0)

    for n, copy in enumerate(copies):
        copy.wait_recv()
        total = total + acr[n]
    misfit = pair_scale() * total - value
    residual = weight * jnp.tanh(misfit * (1.0 / saturation))
    for link in links:
        residual = residual + jnp.where(link >= 0, take(residual, jnp.maximum(link, 0)), 0.0)
    resb[own] = residual
    copies = []
    for n, (dz, dx) in enumerate(SPREAD):
        copy = pltpu.make_async_remote_copy(
            resb.at[own], resb.at[own], ss.at[n], sr.at[n],
            device_id=in_mem(dz, dx), device_id_type=MESH,
        )
        copy.start()
        copies.append(copy)
    sends.extend(copies)
    for copy in copies:
        copy.wait_recv()

    def place(k, carry):
        given = resb[k]
        for half in range(2):
            rows = pl.ds(pl.multiple_of(half * 128 + k * 16, 16), 16)
            for side in range(2):
                lanes = slice(side * 128, side * 128 + 128)
                at = first[rows, lanes]
                forcing = jnp.where(at >= 0, take(given, jnp.maximum(at, 0)), 0.0)
                for m in range(2):
                    high, low = split(ens[m, rows, lanes].astype(f32) * forcing)
                    vhi[m, rows, lanes] = high
                    vlo[m, rows, lanes] = low
        return carry

    lax.fori_loop(0, 8, place, 0)
    copies = begin(1)
    update = finish(1, copies)
    for m in range(2):
        ctl[m] = ctl[m] + w0[m] + update[:, m * TILE : (m + 1) * TILE]
    store = pltpu.make_async_copy(ctl, out, load_sem.at[0])
    store.start()
    for copy in sends:
        copy.wait_send()
    store.wait()


def on_device(control, ensemble, obs_index, obs_value, obs_weight):
    vmem, dma = pltpu.VMEM, pltpu.SemaphoreType.DMA
    square = (TILE, TILE)
    return pl.pallas_call(
        kernel,
        out_shape=jax.ShapeDtypeStruct((2, TILE, TILE), f32),
        in_specs=[pl.BlockSpec(memory_space=pl.ANY)] * 5,
        out_specs=pl.BlockSpec(memory_space=pl.ANY),
        scratch_shapes=[
            vmem((2,) + square, f32), vmem((2,) + square, bf16), vmem((TILE, OBS), i32),
            vmem((2, 16, OBS), f32), vmem((2, 16, OBS), f32),
            vmem(square, bf16), vmem(square, bf16), vmem((2,) + square, bf16), vmem((2,) + square, bf16),
            vmem((2,) + square, f32), vmem(square, f32), vmem((128, 128), i32), vmem(square, i32),
            vmem((2, 8, 384), f32), vmem((2, 4, 8, 384), f32), vmem((2, 4, 8, 384), f32), vmem((2, 15, 8, 128), f32),
            vmem((8, 16, 128), f32), vmem((7, 16, 128), f32), vmem((16, 128), f32), vmem((3, 16, 128), f32), vmem((8, 16, 128), f32),
            dma((7,)), dma((2, 15)), dma((2, 15)), dma((7,)), dma((7,)), dma((3,)), dma((3,)), dma((7,)), dma((7,)),
        ],
        compiler_params=pltpu.CompilerParams(collective_id=0, has_side_effects=True),
    )(control, ensemble, obs_index, obs_value, obs_weight)


def solution(mesh):
    return jax.shard_map(
        on_device,
        mesh=mesh,
        in_specs=(
            P("mem", "gx", "gy"),
            P("mem", "gx", "gy"),
            P("gx", "gy"),
            P("gx", "gy"),
            P("gx", "gy"),
        ),
        out_specs=P("mem", "gx", "gy"),
        check_vma=False,
    )
```

```python
import functools
import math

import jax
import jax.numpy as jnp
from jax import lax
from jax.experimental import pallas as pl
from jax.experimental.pallas import tpu as pltpu
from jax.sharding import PartitionSpec as P

LEN = 400
TILE = 256
GRID = 4
RING = 16
NX = GRID * TILE
OBS = 64
saturation = 1.5
MESH = pl.DeviceIdType.MESH
f32 = jnp.float32
bf16 = jnp.bfloat16
i32 = jnp.int32
FAR = 1 << 20

CORNERS = [(dx, dy) for dy in (2, 1, 3) for dx in (2, 3, 1)]
LINES = [(0, 2), (0, 1), (0, 3), (2, 0), (3, 0), (1, 0)]
AROUND = [(dz, dx) for dz in (8, -7, 7, -6, 6, -5, 5, -4, 4, -3, 3, -2, 2, -1, 1, 0) for dx in (1, 0)][:-1]
BACK = [(dz, dx) for dz in (-4, -3, 3, -2, 2, -1, 1, 0) for dx in (1, 0)][:-1]
NEAR = [(dz, dx) for dz in (-2, 2, -1, 1, 0) for dx in (1, 0)][:-1]
PIECES = 16
ROWS = 8


def pair_scale():
    decay_rate = math.exp(-1.0 / LEN)
    return (1.0 - decay_rate * decay_rate) / (1.0 + decay_rate * decay_rate)


def decay(steps):
    return jnp.exp(steps.astype(f32) * (-1.0 / LEN))


def split(x):
    high = x.astype(bf16)
    return high, (x - high.astype(f32)).astype(bf16)


def dot(a, b, left=1, right=0):
    return lax.dot_general(a, b, (((left,), (right,)), ((), ())), preferred_element_type=f32)


def take(x, lanes):
    return jnp.take_along_axis(x, lanes, axis=1)


def iota(shape, dim):
    return lax.broadcasted_iota(i32, shape, dim)


def in_plane(dx, dy):
    return {
        "gx": lax.rem(lax.axis_index("gx") + dx, GRID),
        "gy": lax.rem(lax.axis_index("gy") + dy, GRID),
    }


def in_mem(dz, dx):
    mem = lax.axis_index("mem")
    z, half = lax.rem(mem, RING), mem // RING
    return {"mem": lax.rem(half + dx, 2) * RING + lax.rem(z + dz + RING, RING)}


def piece_of(dz, dx):
    mem = lax.axis_index("mem")
    z, half = lax.rem(mem, RING), mem // RING
    piece = lax.rem(z + dz + RING, PIECES // 2) * 2 + lax.rem(half + dx, 2)
    return pl.ds(pl.multiple_of(piece * ROWS, ROWS), ROWS)


def send(src, dst, send_sem, recv_sem, peer):
    pltpu.make_async_remote_copy(
        src, dst, send_sem, recv_sem, device_id=peer, device_id_type=MESH
    ).start()


def arrived(ref, sem):
    pltpu.make_async_copy(ref, ref, sem).wait()


def coefficients(axis, d, even, shape):
    me = lax.axis_index(axis)
    it = lax.rem(me - d + GRID, GRID)
    before = jnp.where(it < me, TILE * (me - it - 1) + 1, FAR)
    after = jnp.where(it > me, TILE * (it - me - 1) + 1, FAR)
    ends = 2 * NX - TILE * (me + it + 2) + 2
    own = decay(jnp.where(even, before, after))
    above = jnp.where(even, 0.0, -decay(jnp.full(shape, ends, i32)))
    return own, above


def kernel(
    control, ensemble, obs_index, obs_value, obs_weight, field, side_a, side_b,
    ctl, ens, idx, val, wgt, thi, tlo, vhi, vlo, w0, part, idxp, first,
    msg, lines, corners, pkb, gat, resb, valp, wgtp,
    load_sem, line_send, line_recv, corner_send, corner_recv, sum_send, sum_recv, back_send, back_recv,
    second, third,
):
    loads = [
        pltpu.make_async_copy(control, ctl, load_sem.at[0]),
        pltpu.make_async_copy(obs_index, idx, load_sem.at[1]),
        pltpu.make_async_copy(ensemble, ens, load_sem.at[2]),
        pltpu.make_async_copy(obs_value, val, load_sem.at[3]),
        pltpu.make_async_copy(obs_weight, wgt, load_sem.at[4]),
    ]
    for copy in loads:
        copy.start()
    barrier = pltpu.get_barrier_semaphore()
    peers = [in_plane(*o) for o in CORNERS + LINES] + [in_mem(*o) for o in NEAR]
    for peer in peers:
        pl.semaphore_signal(barrier, 1, device_id=peer, device_id_type=MESH)

    own = piece_of(0, 0)
    square = (TILE, TILE)
    table = decay(jnp.abs(iota(square, 0) - iota(square, 1)))
    high, low = split(table)
    thi[...] = high
    tlo[...] = low
    wide = (8, TILE)
    row, column = iota(wide, 0), iota(wide, 1)
    even = (row & 1) == 0
    ends = decay(jnp.where(even, TILE - 1 - column, column))
    starts = decay(jnp.where(even, column, TILE - 1 - column))
    f_row, b_row = ends[0:1], ends[1:2]
    ends_hi = ends.astype(bf16).astype(f32)
    ends16 = jnp.concatenate([ends_hi, ends - ends_hi], axis=0).astype(bf16)
    narrow = (8, 128)
    lane = iota(narrow, 1)
    left = lane < 64
    left16 = iota((16, 128), 1) < 64
    cx = [coefficients("gx", d, even, wide) for d in range(GRID)]
    cy = [coefficients("gy", d, even, wide) for d in range(GRID)]
    cl = [coefficients("gy", d, left, narrow) for d in range(GRID)]

    def fold(x):
        return x[0:8] + x[8:16]

    def summarize(turn):
        sums = []
        for side in range(2):
            for m in range(2):
                sums.append(fold(dot(ends16, vhi[m], 1, side) + dot(ends16, vlo[m], 1, side)))
        x = jnp.where(row < 2, sums[0], jnp.where(row < 4, sums[1], jnp.where(row < 6, sums[2], sums[3])))
        x_hi = x.astype(bf16).astype(f32)
        x16 = jnp.concatenate([x_hi, x - x_hi], axis=0).astype(bf16)
        corner_f = jnp.sum(x * f_row, axis=1, keepdims=True)
        corner_b = jnp.sum(x * b_row, axis=1, keepdims=True)
        msg[turn, :, 0:TILE] = fold(dot(x16, thi[...]) + dot(x16, tlo[...]))
        msg[turn, :, TILE:] = jnp.where(left, corner_f, corner_b)

    def share(turn):
        for n, o in enumerate(CORNERS):
            send(
                msg.at[turn, :, pl.ds(TILE, 128)], corners.at[turn, n],
                corner_send.at[turn], corner_recv.at[turn], in_plane(*o),
            )
        for n, o in enumerate(LINES):
            send(msg.at[turn], lines.at[turn, n], line_send.at[turn], line_recv.at[turn], in_plane(*o))

    def local(m):
        u = dot(thi[...], vhi[m]) + dot(tlo[...], vhi[m]) + dot(thi[...], vlo[m])
        uhi, ulo = split(u)
        return dot(uhi, thi[...]) + dot(ulo, thi[...]) + dot(uhi, tlo[...])

    def remote(turn):
        arrived(corners.at[turn], corner_recv.at[turn])
        arrived(lines.at[turn], line_recv.at[turn])

        def block(dx, dy):
            if (dx, dy) == (0, 0):
                return msg[turn]
            return lines[turn, LINES.index((dx, dy))]

        def weigh(c, x):
            return c[0] * x + c[1] * pltpu.roll(x, 1, 0)

        xs, ys, corner = 0.0, 0.0, 0.0
        for d in range(GRID):
            xs = xs + weigh(cx[d], block(d, 0)[:, 0:TILE])
            ys = ys + weigh(cy[d], block(0, d)[:, 0:TILE])
        for dy in range(GRID):
            over_x = 0.0
            for dx in range(GRID):
                if dx and dy:
                    g = corners[turn, CORNERS.index((dx, dy))]
                else:
                    g = block(dx, dy)[:, TILE:]
                over_x = over_x + weigh((cx[dx][0][:, 0:128], cx[dx][1][:, 0:128]), g)
            corner = corner + cl[dy][0] * over_x + cl[dy][1] * pltpu.roll(over_x, 64, 1)
        ab = jnp.where(row < 4, xs + corner[:, 0:1] * b_row + corner[:, 64:65] * f_row, ys)
        a = jnp.where(row < 4, starts, ab)
        b = jnp.where(row < 4, ab, starts)
        b = jnp.concatenate([jnp.where((row & 2) == 0, b, 0.0), jnp.where((row & 2) == 0, 0.0, b)], axis=1)
        a_hi, b_hi = a.astype(bf16).astype(f32), b.astype(bf16).astype(f32)
        a_lo, b_lo = a - a_hi, b - b_hi
        a = jnp.concatenate([a_hi, a_hi, a_lo, a_lo], axis=0).astype(bf16)
        b = jnp.concatenate([b_hi, b_lo, b_hi, b_lo], axis=0).astype(bf16)
        return a, b

    def pack(ref):
        return jnp.concatenate([ref[:, 0:128], ref[:, 128:256]], axis=0).T

    loads[0].wait()
    for m in range(2):
        high, low = split(ctl[m])
        vhi[m] = high
        vlo[m] = low
    summarize(0)
    pl.semaphore_wait(barrier, len(peers))
    for dz in (-2, 2):
        pl.semaphore_signal(second, 1, device_id=in_mem(dz, 0), device_id_type=MESH)
    share(0)
    for m in range(2):
        w0[m] = local(m)
    loads[1].wait()
    idxp[...] = pack(idx)
    loads[2].wait()
    pl.semaphore_wait(second, 2)
    for dz in (-4, 4):
        pl.semaphore_signal(third, 1, device_id=in_mem(dz, 0), device_id_type=MESH)
    a, b = remote(0)
    update = dot(a, b, 0, 0)
    part[...] = (
        ens[0].astype(f32) * (w0[0] + update[:, 0:TILE])
        + ens[1].astype(f32) * (w0[1] + update[:, TILE:])
    )

    def pick(k, carry):
        top = pl.ds(pl.multiple_of(k * 16, 16), 16)
        bottom = pl.ds(pl.multiple_of(128 + k * 16, 16), 16)
        at = idxp[top, :]
        low = at & 127
        upper = at >= 128
        above = jnp.where(upper, take(part[top, 128:256], low), take(part[top, 0:128], low))
        below = jnp.where(upper, take(part[bottom, 128:256], low), take(part[bottom, 0:128], low))
        pkb[top, :] = jnp.where(left16, above, below)
        return carry

    lax.fori_loop(0, 8, pick, 0, unroll=4)

    pl.semaphore_wait(third, 2)
    for n, o in enumerate(AROUND):
        send(pkb.at[piece_of(*o)], gat.at[n], sum_send, sum_recv, in_mem(*o))

    at = idxp[own, :]
    link = jnp.full(narrow, -1, i32)
    for j in range(OBS):
        here = jnp.where(left, at[:, j : j + 1], at[:, OBS + j : OBS + j + 1])
        there = jnp.where(left, j, OBS + j)
        link = jnp.where((here == at) & (lane > there), there, link)
    links = []
    for level in range(6):
        links.append(link)
        link = jnp.where(link >= 0, take(link, jnp.maximum(link, 0)), -1)
    loads[3].wait()
    loads[4].wait()
    valp[...] = pack(val)
    wgtp[...] = pack(wgt)
    value = valp[own, :]
    weight = wgtp[own, :] * (saturation * pair_scale())

    def find(k, carry):
        at = idxp[pl.ds(pl.multiple_of(k * 8, 8), 8), :]
        found = [jnp.full(narrow, -1, i32) for _ in range(4)]
        for j in range(OBS):
            for half in range(2):
                here = jnp.broadcast_to(at[:, half * OBS + j : half * OBS + j + 1], narrow)
                found[half * 2] = jnp.where(here == lane, half * OBS + j, found[half * 2])
                found[half * 2 + 1] = jnp.where(here == lane + 128, half * OBS + j, found[half * 2 + 1])
        for half in range(2):
            rows = pl.ds(pl.multiple_of(half * 128 + k * 8, 8), 8)
            first[rows, 0:128] = found[half * 2]
            first[rows, 128:256] = found[half * 2 + 1]
        return carry

    lax.fori_loop(0, 16, find, 0)

    arrived(gat, sum_recv)
    total = pkb[own, :] + jnp.sum(gat[...], axis=0)
    misfit = pair_scale() * total - value
    residual = weight * jnp.tanh(misfit * (1.0 / saturation))
    for link in links:
        residual = residual + jnp.where(link >= 0, take(residual, jnp.maximum(link, 0)), 0.0)
    resb[own, :] = residual
    for o in BACK:
        send(resb.at[own], resb.at[own], back_send, back_recv, in_mem(*o))
    others = resb.at[pl.ds(0, ROWS * len(BACK))]
    arrived(others, back_recv)

    def place(k, carry):
        given = resb[pl.ds(pl.multiple_of(k * 16, 16), 16), :]
        for half in range(2):
            rows = pl.ds(pl.multiple_of(half * 128 + k * 16, 16), 16)
            for side in range(2):
                lanes = slice(side * 128, side * 128 + 128)
                at = first[rows, lanes]
                forcing = jnp.where(at >= 0, take(given, jnp.maximum(at, 0)), 0.0)
                for m in range(2):
                    high, low = split(ens[m, rows, lanes].astype(f32) * forcing)
                    vhi[m, rows, lanes] = high
                    vlo[m, rows, lanes] = low
        return carry

    lax.fori_loop(0, 8, place, 0, unroll=4)
    summarize(1)
    share(1)
    for m in range(2):
        field[m] = ctl[m] + local(m)
    arrived(gat, sum_send)
    arrived(others, back_send)
    for turn in range(2):
        arrived(corners.at[turn], corner_send.at[turn])
        arrived(lines.at[turn], line_send.at[turn])
    a, b = remote(1)
    side_a[...] = a
    side_b[...] = b


def join(field, side_a, side_b, out, both, sem):
    copies = []
    for half in range(2):
        rows = slice(half * 128, half * 128 + 128)
        update = dot(side_a[:, rows], side_b[...], 0, 0)
        for m in range(2):
            both[m, rows, :] = field[m, rows, :] + update[:, m * TILE : (m + 1) * TILE]
            copy = pltpu.make_async_copy(both.at[m, rows, :], out.at[m, rows, :], sem.at[half, m])
            copy.start()
            copies.append(copy)
    for copy in copies:
        copy.wait()


def on_device(control, ensemble, obs_index, obs_value, obs_weight):
    vmem, dma = pltpu.VMEM, pltpu.SemaphoreType.DMA
    square = (TILE, TILE)
    packed = (128, 128)
    field, side_a, side_b = pl.pallas_call(
        kernel,
        out_shape=[vmem((2,) + square, f32), vmem((32, TILE), bf16), vmem((32, 2 * TILE), bf16)],
        in_specs=[pl.BlockSpec(memory_space=pltpu.HBM)] * 5,
        out_specs=[pl.BlockSpec(memory_space=vmem)] * 3,
        scratch_shapes=[
            vmem((2,) + square, f32), vmem((2,) + square, bf16),
            vmem((OBS, TILE), i32), vmem((OBS, TILE), f32), vmem((OBS, TILE), f32),
            vmem(square, bf16), vmem(square, bf16), vmem((2,) + square, bf16), vmem((2,) + square, bf16),
            vmem((2,) + square, f32), vmem(square, f32), vmem(packed, i32), vmem(square, i32),
            vmem((2, 8, 384), f32), vmem((2, len(LINES), 8, 384), f32), vmem((2, len(CORNERS), 8, 128), f32),
            vmem(packed, f32), vmem((len(AROUND), ROWS, 128), f32), vmem(packed, f32), vmem(packed, f32), vmem(packed, f32),
            dma((5,)), dma((2,)), dma((2,)), dma((2,)), dma((2,)), dma, dma, dma, dma,
            pltpu.SemaphoreType.REGULAR, pltpu.SemaphoreType.REGULAR,
        ],
        compiler_params=pltpu.CompilerParams(
            collective_id=0, has_side_effects=True, vmem_limit_bytes=24 << 20
        ),
    )(control, ensemble, obs_index.T, obs_value.T, obs_weight.T)
    return pl.pallas_call(
        join,
        out_shape=jax.ShapeDtypeStruct((2,) + square, f32),
        in_specs=[pl.BlockSpec(memory_space=vmem)] * 3,
        out_specs=pl.BlockSpec(memory_space=pl.ANY),
        scratch_shapes=[vmem((2,) + square, f32), dma((2, 2))],
        compiler_params=pltpu.CompilerParams(vmem_limit_bytes=8 << 20),
    )(field, side_a, side_b)


def solution(mesh):
    return jax.shard_map(
        on_device,
        mesh=mesh,
        in_specs=(
            P("mem", "gx", "gy"),
            P("mem", "gx", "gy"),
            P("gx", "gy"),
            P("gx", "gy"),
            P("gx", "gy"),
        ),
        out_specs=P("mem", "gx", "gy"),
        check_vma=False,
    )
```

```python
import functools
import math

import jax
import jax.numpy as jnp
from jax import lax
from jax.experimental import pallas as pl
from jax.experimental.pallas import tpu as pltpu
from jax.sharding import PartitionSpec as P

LEN = 400
TILE = 256
GRID = 4
RING = 16
NX = GRID * TILE
OBS = 64
saturation = 1.5
MESH = pl.DeviceIdType.MESH
f32 = jnp.float32
bf16 = jnp.bfloat16
i32 = jnp.int32
FAR = 1 << 20

CORNERS = [(dx, dy) for dy in (2, 1, 3) for dx in (2, 3, 1)]
LINES = [(0, 2), (0, 1), (0, 3), (2, 0), (3, 0), (1, 0)]
AROUND = [(dz, dx) for dz in (8, -7, 7, -6, 6, -5, 5, -4, 4, -3, 3, -2, 2, -1, 1, 0) for dx in (1, 0)][:-1]
BACK = [(dz, dx) for dz in (-4, -3, 3, -2, 2, -1, 1, 0) for dx in (1, 0)][:-1]
NEAR = [(dz, dx) for dz in (-2, 2, -1, 1, 0) for dx in (1, 0)][:-1]
PIECES = 16
ROWS = 8


def pair_scale():
    decay_rate = math.exp(-1.0 / LEN)
    return (1.0 - decay_rate * decay_rate) / (1.0 + decay_rate * decay_rate)


def decay(steps):
    return jnp.exp(steps.astype(f32) * (-1.0 / LEN))


def split(x):
    high = x.astype(bf16)
    return high, (x - high.astype(f32)).astype(bf16)


def dot(a, b, left=1, right=0):
    return lax.dot_general(a, b, (((left,), (right,)), ((), ())), preferred_element_type=f32)


def take(x, lanes):
    return jnp.take_along_axis(x, lanes, axis=1)


def iota(shape, dim):
    return lax.broadcasted_iota(i32, shape, dim)


def in_plane(dx, dy):
    return {
        "gx": lax.rem(lax.axis_index("gx") + dx, GRID),
        "gy": lax.rem(lax.axis_index("gy") + dy, GRID),
    }


def in_mem(dz, dx):
    mem = lax.axis_index("mem")
    z, half = lax.rem(mem, RING), mem // RING
    return {"mem": lax.rem(half + dx, 2) * RING + lax.rem(z + dz + RING, RING)}


def piece_of(dz, dx):
    mem = lax.axis_index("mem")
    z, half = lax.rem(mem, RING), mem // RING
    piece = lax.rem(z + dz + RING, PIECES // 2) * 2 + lax.rem(half + dx, 2)
    return pl.ds(pl.multiple_of(piece * ROWS, ROWS), ROWS)


def send(src, dst, send_sem, recv_sem, peer):
    pltpu.make_async_remote_copy(
        src, dst, send_sem, recv_sem, device_id=peer, device_id_type=MESH
    ).start()


def arrived(ref, sem):
    pltpu.make_async_copy(ref, ref, sem).wait()


def coefficients(axis, d, even, shape):
    me = lax.axis_index(axis)
    it = lax.rem(me - d + GRID, GRID)
    before = jnp.where(it < me, TILE * (me - it - 1) + 1, FAR)
    after = jnp.where(it > me, TILE * (it - me - 1) + 1, FAR)
    ends = 2 * NX - TILE * (me + it + 2) + 2
    own = decay(jnp.where(even, before, after))
    above = jnp.where(even, 0.0, -decay(jnp.full(shape, ends, i32)))
    return own, above


def kernel(
    control, ensemble, obs_index, obs_value, obs_weight, field, side_a, side_b,
    ctl, ens, idx, val, wgt, thi, tlo, vhi, vlo, w0, part, idxp, first,
    msg, lines, corners, pkb, gat, resb, valp, wgtp,
    load_sem, line_send, line_recv, corner_send, corner_recv, sum_send, sum_recv, back_send, back_recv,
    second, third,
):
    loads = [
        pltpu.make_async_copy(control, ctl, load_sem.at[0]),
        pltpu.make_async_copy(obs_index, idx, load_sem.at[1]),
        pltpu.make_async_copy(ensemble, ens, load_sem.at[2]),
        pltpu.make_async_copy(obs_value, val, load_sem.at[3]),
        pltpu.make_async_copy(obs_weight, wgt, load_sem.at[4]),
    ]
    for copy in loads:
        copy.start()
    barrier = pltpu.get_barrier_semaphore()
    peers = [in_plane(*o) for o in CORNERS + LINES] + [in_mem(*o) for o in NEAR]
    for peer in peers:
        pl.semaphore_signal(barrier, 1, device_id=peer, device_id_type=MESH)

    own = piece_of(0, 0)
    square = (TILE, TILE)
    table = decay(jnp.abs(iota(square, 0) - iota(square, 1)))
    high, low = split(table)
    thi[...] = high
    tlo[...] = low
    wide = (8, TILE)
    row, column = iota(wide, 0), iota(wide, 1)
    even = (row & 1) == 0
    ends = decay(jnp.where(even, TILE - 1 - column, column))
    starts = decay(jnp.where(even, column, TILE - 1 - column))
    f_row, b_row = ends[0:1], ends[1:2]
    ends_hi = ends.astype(bf16).astype(f32)
    ends16 = jnp.concatenate([ends_hi, ends - ends_hi], axis=0).astype(bf16)
    narrow = (8, 128)
    lane = iota(narrow, 1)
    left = lane < 64
    left16 = iota((16, 128), 1) < 64
    cx = [coefficients("gx", d, even, wide) for d in range(GRID)]
    cy = [coefficients("gy", d, even, wide) for d in range(GRID)]
    cl = [coefficients("gy", d, left, narrow) for d in range(GRID)]

    def fold(x):
        return x[0:8] + x[8:16]

    def summarize(turn):
        sums = []
        for side in range(2):
            for m in range(2):
                sums.append(fold(dot(ends16, vhi[m], 1, side) + dot(ends16, vlo[m], 1, side)))
        x = jnp.where(row < 2, sums[0], jnp.where(row < 4, sums[1], jnp.where(row < 6, sums[2], sums[3])))
        x_hi = x.astype(bf16).astype(f32)
        x16 = jnp.concatenate([x_hi, x - x_hi], axis=0).astype(bf16)
        corner_f = jnp.sum(x * f_row, axis=1, keepdims=True)
        corner_b = jnp.sum(x * b_row, axis=1, keepdims=True)
        msg[turn, :, 0:TILE] = fold(dot(x16, thi[...]) + dot(x16, tlo[...]))
        msg[turn, :, TILE:] = jnp.where(left, corner_f, corner_b)

    def share(turn):
        for n, o in enumerate(CORNERS):
            send(
                msg.at[turn, :, pl.ds(TILE, 128)], corners.at[turn, n],
                corner_send.at[turn], corner_recv.at[turn], in_plane(*o),
            )
        for n, o in enumerate(LINES):
            send(msg.at[turn], lines.at[turn, n], line_send.at[turn], line_recv.at[turn], in_plane(*o))

    def local(m):
        u = dot(thi[...], vhi[m]) + dot(tlo[...], vhi[m]) + dot(thi[...], vlo[m])
        uhi, ulo = split(u)
        return dot(uhi, thi[...]) + dot(ulo, thi[...]) + dot(uhi, tlo[...])

    def remote(turn):
        arrived(corners.at[turn], corner_recv.at[turn])
        arrived(lines.at[turn], line_recv.at[turn])

        def block(dx, dy):
            if (dx, dy) == (0, 0):
                return msg[turn]
            return lines[turn, LINES.index((dx, dy))]

        def weigh(c, x):
            return c[0] * x + c[1] * pltpu.roll(x, 1, 0)

        xs, ys, corner = 0.0, 0.0, 0.0
        for d in range(GRID):
            xs = xs + weigh(cx[d], block(d, 0)[:, 0:TILE])
            ys = ys + weigh(cy[d], block(0, d)[:, 0:TILE])
        for dy in range(GRID):
            over_x = 0.0
            for dx in range(GRID):
                if dx and dy:
                    g = corners[turn, CORNERS.index((dx, dy))]
                else:
                    g = block(dx, dy)[:, TILE:]
                over_x = over_x + weigh((cx[dx][0][:, 0:128], cx[dx][1][:, 0:128]), g)
            corner = corner + cl[dy][0] * over_x + cl[dy][1] * pltpu.roll(over_x, 64, 1)
        ab = jnp.where(row < 4, xs + corner[:, 0:1] * b_row + corner[:, 64:65] * f_row, ys)
        a = jnp.where(row < 4, starts, ab)
        b = jnp.where(row < 4, ab, starts)
        b = jnp.concatenate([jnp.where((row & 2) == 0, b, 0.0), jnp.where((row & 2) == 0, 0.0, b)], axis=1)
        a_hi, b_hi = a.astype(bf16).astype(f32), b.astype(bf16).astype(f32)
        a_lo, b_lo = a - a_hi, b - b_hi
        a = jnp.concatenate([a_hi, a_hi, a_lo, a_lo], axis=0).astype(bf16)
        b = jnp.concatenate([b_hi, b_lo, b_hi, b_lo], axis=0).astype(bf16)
        return a, b

    def pack(ref):
        return jnp.concatenate([ref[:, 0:128], ref[:, 128:256]], axis=0).T

    loads[0].wait()
    for m in range(2):
        high, low = split(ctl[m])
        vhi[m] = high
        vlo[m] = low
    summarize(0)
    pl.semaphore_wait(barrier, len(peers))
    for dz in (-2, 2):
        pl.semaphore_signal(second, 1, device_id=in_mem(dz, 0), device_id_type=MESH)
    share(0)
    for m in range(2):
        w0[m] = local(m)
    loads[1].wait()
    idxp[...] = pack(idx)
    loads[2].wait()
    pl.semaphore_wait(second, 2)
    for dz in (-4, 4):
        pl.semaphore_signal(third, 1, device_id=in_mem(dz, 0), device_id_type=MESH)
    a, b = remote(0)
    update = dot(a, b, 0, 0)
    part[...] = (
        ens[0].astype(f32) * (w0[0] + update[:, 0:TILE])
        + ens[1].astype(f32) * (w0[1] + update[:, TILE:])
    )

    def pick(k, carry):
        top = pl.ds(pl.multiple_of(k * 16, 16), 16)
        bottom = pl.ds(pl.multiple_of(128 + k * 16, 16), 16)
        at = idxp[top, :]
        low = at & 127
        upper = at >= 128
        above = jnp.where(upper, take(part[top, 128:256], low), take(part[top, 0:128], low))
        below = jnp.where(upper, take(part[bottom, 128:256], low), take(part[bottom, 0:128], low))
        pkb[top, :] = jnp.where(left16, above, below)
        return carry

    lax.fori_loop(0, 8, pick, 0, unroll=4)

    pl.semaphore_wait(third, 2)
    for n, o in enumerate(AROUND):
        send(pkb.at[piece_of(*o)], gat.at[n], sum_send, sum_recv, in_mem(*o))

    at = idxp[own, :]
    link = jnp.full(narrow, -1, i32)
    for j in range(OBS):
        here = jnp.where(left, at[:, j : j + 1], at[:, OBS + j : OBS + j + 1])
        there = jnp.where(left, j, OBS + j)
        link = jnp.where((here == at) & (lane > there), there, link)
    links = []
    for level in range(6):
        links.append(link)
        link = jnp.where(link >= 0, take(link, jnp.maximum(link, 0)), -1)
    loads[3].wait()
    loads[4].wait()
    valp[...] = pack(val)
    wgtp[...] = pack(wgt)
    value = valp[own, :]
    weight = wgtp[own, :] * (saturation * pair_scale())

    def find(k, carry):
        at = idxp[pl.ds(pl.multiple_of(k * 8, 8), 8), :]
        found = [jnp.full(narrow, -1, i32) for _ in range(4)]
        for j in range(OBS):
            for half in range(2):
                here = jnp.broadcast_to(at[:, half * OBS + j : half * OBS + j + 1], narrow)
                found[half * 2] = jnp.where(here == lane, half * OBS + j, found[half * 2])
                found[half * 2 + 1] = jnp.where(here == lane + 128, half * OBS + j, found[half * 2 + 1])
        for half in range(2):
            rows = pl.ds(pl.multiple_of(half * 128 + k * 8, 8), 8)
            first[rows, 0:128] = found[half * 2]
            first[rows, 128:256] = found[half * 2 + 1]
        return carry

    lax.fori_loop(0, 16, find, 0)

    arrived(gat, sum_recv)
    total = pkb[own, :] + jnp.sum(gat[...], axis=0)
    misfit = pair_scale() * total - value
    residual = weight * jnp.tanh(misfit * (1.0 / saturation))
    for link in links:
        residual = residual + jnp.where(link >= 0, take(residual, jnp.maximum(link, 0)), 0.0)
    resb[own, :] = residual
    for o in BACK:
        send(resb.at[own], resb.at[own], back_send, back_recv, in_mem(*o))
    others = resb.at[pl.ds(0, ROWS * len(BACK))]
    arrived(others, back_recv)

    def place(k, carry):
        given = resb[pl.ds(pl.multiple_of(k * 16, 16), 16), :]
        for half in range(2):
            rows = pl.ds(pl.multiple_of(half * 128 + k * 16, 16), 16)
            for side in range(2):
                lanes = slice(side * 128, side * 128 + 128)
                at = first[rows, lanes]
                forcing = jnp.where(at >= 0, take(given, jnp.maximum(at, 0)), 0.0)
                for m in range(2):
                    high, low = split(ens[m, rows, lanes].astype(f32) * forcing)
                    vhi[m, rows, lanes] = high
                    vlo[m, rows, lanes] = low
        return carry

    lax.fori_loop(0, 8, place, 0, unroll=4)
    summarize(1)
    share(1)
    for m in range(2):
        field[m] = ctl[m] + local(m)
    arrived(gat, sum_send)
    arrived(others, back_send)
    for turn in range(2):
        arrived(corners.at[turn], corner_send.at[turn])
        arrived(lines.at[turn], line_send.at[turn])
    a, b = remote(1)
    side_a[...] = a
    side_b[...] = b


def join(field, side_a, side_b, out, both, sem):
    copies = []
    for half in range(2):
        rows = slice(half * 128, half * 128 + 128)
        update = dot(side_a[:, rows], side_b[...], 0, 0)
        for m in range(2):
            both[m, rows, :] = field[m, rows, :] + update[:, m * TILE : (m + 1) * TILE]
            copy = pltpu.make_async_copy(both.at[m, rows, :], out.at[m, rows, :], sem.at[half, m])
            copy.start()
            copies.append(copy)
    for copy in copies:
        copy.wait()


def on_device(control, ensemble, obs_index, obs_value, obs_weight):
    vmem, dma = pltpu.VMEM, pltpu.SemaphoreType.DMA
    square = (TILE, TILE)
    packed = (128, 128)
    field, side_a, side_b = pl.pallas_call(
        kernel,
        out_shape=[vmem((2,) + square, f32), vmem((32, TILE), bf16), vmem((32, 2 * TILE), bf16)],
        in_specs=[pl.BlockSpec(memory_space=pltpu.HBM)] * 5,
        out_specs=[pl.BlockSpec(memory_space=vmem)] * 3,
        scratch_shapes=[
            vmem((2,) + square, f32), vmem((2,) + square, bf16),
            vmem((OBS, TILE), i32), vmem((OBS, TILE), f32), vmem((OBS, TILE), f32),
            vmem(square, bf16), vmem(square, bf16), vmem((2,) + square, bf16), vmem((2,) + square, bf16),
            vmem((2,) + square, f32), vmem(square, f32), vmem(packed, i32), vmem(square, i32),
            vmem((2, 8, 384), f32), vmem((2, len(LINES), 8, 384), f32), vmem((2, len(CORNERS), 8, 128), f32),
            vmem(packed, f32), vmem((len(AROUND), ROWS, 128), f32), vmem(packed, f32), vmem(packed, f32), vmem(packed, f32),
            dma((5,)), dma((2,)), dma((2,)), dma((2,)), dma((2,)), dma, dma, dma, dma,
            pltpu.SemaphoreType.REGULAR, pltpu.SemaphoreType.REGULAR,
        ],
        compiler_params=pltpu.CompilerParams(
            collective_id=0, has_side_effects=True, vmem_limit_bytes=24 << 20
        ),
    )(*(
        pltpu.with_memory_space_constraint(x, pltpu.HBM)
        for x in (control, ensemble, obs_index.T, obs_value.T, obs_weight.T)
    ))
    return pl.pallas_call(
        join,
        out_shape=jax.ShapeDtypeStruct((2,) + square, f32),
        in_specs=[pl.BlockSpec(memory_space=vmem)] * 3,
        out_specs=pl.BlockSpec(memory_space=pl.ANY),
        scratch_shapes=[vmem((2,) + square, f32), dma((2, 2))],
        compiler_params=pltpu.CompilerParams(vmem_limit_bytes=8 << 20),
    )(field, side_a, side_b)


def solution(mesh):
    return jax.shard_map(
        on_device,
        mesh=mesh,
        in_specs=(
            P("mem", "gx", "gy"),
            P("mem", "gx", "gy"),
            P("gx", "gy"),
            P("gx", "gy"),
            P("gx", "gy"),
        ),
        out_specs=P("mem", "gx", "gy"),
        check_vma=False,
    )
```

```python
import functools
import math

import jax
import jax.numpy as jnp
from jax import lax
from jax.experimental import pallas as pl
from jax.experimental.pallas import tpu as pltpu
from jax.sharding import PartitionSpec as P

LEN = 400
TILE = 256
GRID = 4
RING = 16
NX = GRID * TILE
OBS = 64
saturation = 1.5
MESH = pl.DeviceIdType.MESH
f32 = jnp.float32
bf16 = jnp.bfloat16
i32 = jnp.int32
FAR = 1 << 20

CORNERS = [(dx, dy) for dy in (2, 1, 3) for dx in (2, 3, 1)]
LINES = [(0, 2), (0, 1), (0, 3), (2, 0), (3, 0), (1, 0)]
COLUMN = [8, -7, 7, -6, 6, -5, 5, -4, 4, -3, 3, -2, 2, -1, 1]
BACK = [(dz, dx) for dz in (-4, -3, 3, -2, 2, -1, 1, 0) for dx in (1, 0)]
NEAR = [(-4, 0), (4, 0), (-3, 0), (3, 0), (-2, 0), (2, 0), (0, 1), (-1, 0), (1, 0)]
PIECES = 8
ROWS = 16
LEVELS = 6


def pair_scale():
    decay_rate = math.exp(-1.0 / LEN)
    return (1.0 - decay_rate * decay_rate) / (1.0 + decay_rate * decay_rate)


def decay(steps):
    return jnp.exp(steps.astype(f32) * (-1.0 / LEN))


def split(x):
    high = x.astype(bf16)
    return high, (x - high.astype(f32)).astype(bf16)


def dot(a, b, left=1, right=0):
    return lax.dot_general(a, b, (((left,), (right,)), ((), ())), preferred_element_type=f32)


def take(x, lanes):
    return jnp.take_along_axis(x, lanes, axis=1)


def iota(shape, dim):
    return lax.broadcasted_iota(i32, shape, dim)


def in_plane(dx, dy):
    return {
        "gx": lax.rem(lax.axis_index("gx") + dx, GRID),
        "gy": lax.rem(lax.axis_index("gy") + dy, GRID),
    }


def in_mem(dz, dx):
    mem = lax.axis_index("mem")
    z, half = lax.rem(mem, RING), mem // RING
    return {"mem": lax.rem(half + dx, 2) * RING + lax.rem(z + dz + RING, RING)}


def piece_of(dz):
    piece = lax.rem(lax.axis_index("mem") + dz + RING, PIECES)
    return pl.ds(pl.multiple_of(piece * ROWS, ROWS), ROWS)


def send(src, dst, send_sem, recv_sem, peer):
    pltpu.make_async_remote_copy(
        src, dst, send_sem, recv_sem, device_id=peer, device_id_type=MESH
    ).start()


def arrived(ref, sem):
    pltpu.make_async_copy(ref, ref, sem).wait()


def coefficients(axis, d, even, shape):
    me = lax.axis_index(axis)
    it = lax.rem(me - d + GRID, GRID)
    before = jnp.where(it < me, TILE * (me - it - 1) + 1, FAR)
    after = jnp.where(it > me, TILE * (it - me - 1) + 1, FAR)
    ends = 2 * NX - TILE * (me + it + 2) + 2
    own = decay(jnp.where(even, before, after))
    above = jnp.where(even, 0.0, -decay(jnp.full(shape, ends, i32)))
    return own, above


def kernel(
    control, ensemble, obs_index, obs_value, obs_weight, field, side_a, side_b,
    ctl, ens, idx, val, wgt, thi, tlo, vhi, vlo, w0, part, idxp, first, nexts,
    msg, lines, corners, pkb, gat, tot, res, valp, wgtp,
    load_sem, line_send, line_recv, corner_send, corner_recv, sum_send, sum_recv, back_send, back_recv,
    column_in, sibling_in, other_in, all_in,
):
    loads = [
        pltpu.make_async_copy(control.at[0], ctl.at[0], load_sem.at[0]),
        pltpu.make_async_copy(control.at[1], ctl.at[1], load_sem.at[1]),
        pltpu.make_async_copy(obs_index, idx, load_sem.at[2]),
        pltpu.make_async_copy(ensemble, ens, load_sem.at[3]),
        pltpu.make_async_copy(obs_value, val, load_sem.at[4]),
        pltpu.make_async_copy(obs_weight, wgt, load_sem.at[5]),
    ]
    for copy in loads:
        copy.start()
    barrier = pltpu.get_barrier_semaphore()
    peers = [in_mem(*o) for o in NEAR] + [in_plane(*o) for o in CORNERS + LINES]

    def signal(sem, peer):
        pl.semaphore_signal(sem, 1, device_id=peer, device_id_type=MESH)

    for peer in peers:
        signal(barrier, peer)
    gx = lax.axis_index("gx")
    core = lax.rem(gx, 2)
    half = lax.axis_index("mem") // RING
    sibling = {"gx": gx + 1 - 2 * core}

    own = piece_of(0)
    square = (TILE, TILE)
    table = decay(jnp.abs(iota(square, 0) - iota(square, 1)))
    high, low = split(table)
    thi[...] = high
    tlo[...] = low
    wide = (8, TILE)
    row, column = iota(wide, 0), iota(wide, 1)
    even = (row & 1) == 0
    ends = decay(jnp.where(even, TILE - 1 - column, column))
    starts = decay(jnp.where(even, column, TILE - 1 - column))
    f_row, b_row = ends[0:1], ends[1:2]
    ends_hi = ends.astype(bf16).astype(f32)
    ends16 = jnp.concatenate([ends_hi, ends - ends_hi], axis=0).astype(bf16)
    narrow = (8, 128)
    lane = iota(narrow, 1)
    left = lane < 64
    left16 = iota((16, 128), 1) < 64
    cx = [coefficients("gx", d, even, wide) for d in range(GRID)]
    cy = [coefficients("gy", d, even, wide) for d in range(GRID)]
    cl = [coefficients("gy", d, left, narrow) for d in range(GRID)]

    def fold(x):
        return x[0:8] + x[8:16]

    def summarize(turn):
        over_x, over_y = [], []
        for m in range(2):
            if turn == 0:
                loads[m].wait()
                high, low = split(ctl[m])
                vhi[m] = high
                vlo[m] = low
            for side, sums in enumerate((over_x, over_y)):
                sums.append(fold(dot(ends16, vhi[m], 1, side) + dot(ends16, vlo[m], 1, side)))
        sums = over_x + over_y
        x = jnp.where(row < 2, sums[0], jnp.where(row < 4, sums[1], jnp.where(row < 6, sums[2], sums[3])))
        x_hi = x.astype(bf16).astype(f32)
        x16 = jnp.concatenate([x_hi, x - x_hi], axis=0).astype(bf16)
        corner_f = jnp.sum(x * f_row, axis=1, keepdims=True)
        corner_b = jnp.sum(x * b_row, axis=1, keepdims=True)
        msg[turn, :, 0:TILE] = fold(dot(x16, thi[...]) + dot(x16, tlo[...]))
        msg[turn, :, TILE:] = jnp.where(left, corner_f, corner_b)

    def share(turn):
        for n, o in enumerate(CORNERS):
            send(
                msg.at[turn, :, pl.ds(TILE, 128)], corners.at[turn, n],
                corner_send.at[turn], corner_recv.at[turn], in_plane(*o),
            )
        for n, o in enumerate(LINES):
            send(msg.at[turn], lines.at[turn, n], line_send.at[turn], line_recv.at[turn], in_plane(*o))

    def local(m):
        u = dot(thi[...], vhi[m]) + dot(tlo[...], vhi[m]) + dot(thi[...], vlo[m])
        uhi, ulo = split(u)
        return dot(uhi, thi[...]) + dot(ulo, thi[...]) + dot(uhi, tlo[...])

    def remote(turn):
        arrived(corners.at[turn], corner_recv.at[turn])
        arrived(lines.at[turn], line_recv.at[turn])

        def block(dx, dy):
            if (dx, dy) == (0, 0):
                return msg[turn]
            return lines[turn, LINES.index((dx, dy))]

        def weigh(c, x):
            return c[0] * x + c[1] * pltpu.roll(x, 1, 0)

        xs, ys, corner = 0.0, 0.0, 0.0
        for d in range(GRID):
            xs = xs + weigh(cx[d], block(d, 0)[:, 0:TILE])
            ys = ys + weigh(cy[d], block(0, d)[:, 0:TILE])
        for dy in range(GRID):
            over_x = 0.0
            for dx in range(GRID):
                if dx and dy:
                    g = corners[turn, CORNERS.index((dx, dy))]
                else:
                    g = block(dx, dy)[:, TILE:]
                over_x = over_x + weigh((cx[dx][0][:, 0:128], cx[dx][1][:, 0:128]), g)
            corner = corner + cl[dy][0] * over_x + cl[dy][1] * pltpu.roll(over_x, 64, 1)
        ab = jnp.where(row < 4, xs + corner[:, 0:1] * b_row + corner[:, 64:65] * f_row, ys)
        a = jnp.where(row < 4, starts, ab)
        b = jnp.where(row < 4, ab, starts)
        b = jnp.concatenate([jnp.where((row & 2) == 0, b, 0.0), jnp.where((row & 2) == 0, 0.0, b)], axis=1)
        a_hi, b_hi = a.astype(bf16).astype(f32), b.astype(bf16).astype(f32)
        a_lo, b_lo = a - a_hi, b - b_hi
        a = jnp.concatenate([a_hi, a_hi, a_lo, a_lo], axis=0).astype(bf16)
        b = jnp.concatenate([b_hi, b_lo, b_hi, b_lo], axis=0).astype(bf16)
        return a, b

    def pack(ref):
        return jnp.concatenate([ref[:, 0:128], ref[:, 128:256]], axis=0).T

    summarize(0)
    pl.semaphore_wait(barrier, len(peers))
    for dz in (-4, 4):
        signal(column_in, in_mem(dz, 0))
    share(0)
    for m in range(2):
        w0[m] = local(m)
    loads[2].wait()
    idxp[...] = pack(idx)
    loads[3].wait()
    pl.semaphore_wait(column_in, 2)
    signal(sibling_in, sibling)
    signal(other_in, in_mem(0, 1))
    a, b = remote(0)
    update = dot(a, b, 0, 0)
    part[...] = (
        ens[0].astype(f32) * (w0[0] + update[:, 0:TILE])
        + ens[1].astype(f32) * (w0[1] + update[:, TILE:])
    )

    def pick(k, carry):
        top = pl.ds(pl.multiple_of(k * 16, 16), 16)
        bottom = pl.ds(pl.multiple_of(128 + k * 16, 16), 16)
        at = idxp[top, :]
        low = at & 127
        upper = at >= 128
        above = jnp.where(upper, take(part[top, 128:256], low), take(part[top, 0:128], low))
        below = jnp.where(upper, take(part[bottom, 128:256], low), take(part[bottom, 0:128], low))
        pkb[top, :] = jnp.where(left16, above, below)
        return carry

    lax.fori_loop(0, 8, pick, 0, unroll=4)

    pl.semaphore_wait(sibling_in, 1)
    for n, dz in enumerate(COLUMN):
        send(
            pkb.at[piece_of(dz)], gat.at[core, n], sum_send, sum_recv.at[core],
            in_mem(dz, 0) | {"gx": gx + 1 - core},
        )

    @pl.when(core == 0)
    def _():
        send(pkb.at[own], gat.at[0, len(COLUMN)], sum_send, sum_recv.at[0], sibling)

    @pl.when(core == 1)
    def _():
        gat[1, len(COLUMN)] = pkb[own, :]

    def find(k, carry):
        rows = pl.ds(pl.multiple_of((k // 2) * 128, 128), 128)
        lanes = pl.ds(pl.multiple_of((k % 2) * 128, 128), 128)
        cell = iota((128, 128), 0) + (k % 2) * 128
        found = jnp.full((128, 128), -1, i32)
        for j in range(OBS):
            found = jnp.where(idx[j : j + 1, rows] == cell, (k // 2) * OBS + j, found)
        first[rows, lanes] = found.T
        return carry

    lax.fori_loop(0, 4, find, 0)
    level = iota(narrow, 0)
    link = []
    for side in range(2):
        at = [idx[8 * t : 8 * t + 8, side * 128 : side * 128 + 128] for t in range(8)]
        found = [jnp.full(narrow, -1, i32) for t in range(8)]
        for j in range(OBS):
            here = at[j // 8][j % 8 : j % 8 + 1]
            for t in range(j // 8, 8):
                hit = at[t] == here
                if t == j // 8:
                    hit = hit & (level > j % 8)
                found[t] = jnp.where(hit, side * OBS + j, found[t])
        link += found
    link = jnp.concatenate(link, axis=0).T
    for n in range(LEVELS):
        nexts[n] = link
        link = jnp.where(link >= 0, take(link, jnp.maximum(link, 0)), -1)
    loads[4].wait()
    loads[5].wait()
    valp[...] = pack(val) * (1.0 / saturation)
    wgtp[...] = pack(wgt) * (saturation * pair_scale())
    pl.semaphore_wait(other_in, 1)
    signal(all_in, sibling)
    pl.semaphore_wait(all_in, 1)

    @pl.when(core == 1)
    def _():
        for c in range(2):
            arrived(gat.at[c, pl.ds(0, len(COLUMN) + 1 - c)], sum_recv.at[c])
            tot[c] = jnp.sum(gat[c], axis=0)
            for o in BACK:
                if o != (0, 0):
                    send(tot.at[c], res.at[half, own], back_send.at[c], back_recv, in_mem(*o) | {"gx": gx - 1 + c})
                elif c == 0:
                    send(tot.at[c], res.at[half, own], back_send.at[c], back_recv, sibling)
        res[half, own, :] = tot[1]
        arrived(gat.at[1, pl.ds(0, len(COLUMN))], back_recv)

    @pl.when(core == 0)
    def _():
        arrived(res, back_recv)

    total = res[0] + res[1]
    residual = wgtp[...] * jnp.tanh(total * (pair_scale() / saturation) - valp[...])
    for n in range(LEVELS):
        link = nexts[n]
        residual = residual + jnp.where(link >= 0, take(residual, jnp.maximum(link, 0)), 0.0)
    part[0:128, 0:128] = residual

    def place(k, carry):
        given = part[pl.ds(pl.multiple_of(k * 16, 16), 16), 0:128]
        for half in range(2):
            rows = pl.ds(pl.multiple_of(half * 128 + k * 16, 16), 16)
            for side in range(2):
                lanes = slice(side * 128, side * 128 + 128)
                at = first[rows, lanes]
                forcing = jnp.where(at >= 0, take(given, jnp.maximum(at, 0)), 0.0)
                for m in range(2):
                    high, low = split(ens[m, rows, lanes].astype(f32) * forcing)
                    vhi[m, rows, lanes] = high
                    vlo[m, rows, lanes] = low
        return carry

    lax.fori_loop(0, 8, place, 0, unroll=4)
    summarize(1)
    share(1)
    for m in range(2):
        field[m] = ctl[m] + local(m)

    @pl.when(core == 0)
    def _():
        arrived(gat.at[0], sum_send)

    @pl.when(core == 1)
    def _():
        arrived(gat.at[1, pl.ds(0, len(COLUMN))], sum_send)
        for c in range(2):
            arrived(gat.at[c, pl.ds(0, len(COLUMN) + 1 - c)], back_send.at[c])

    for turn in range(2):
        arrived(corners.at[turn], corner_send.at[turn])
        arrived(lines.at[turn], line_send.at[turn])
    a, b = remote(1)
    side_a[...] = a
    side_b[...] = b


def join(field, side_a, side_b, out, both, sem):
    copies = []
    for quarter in range(4):
        rows = slice(quarter * 64, quarter * 64 + 64)
        update = dot(side_a[:, rows], side_b[...], 0, 0)
        for m in range(2):
            both[m, rows, :] = field[m, rows, :] + update[:, m * TILE : (m + 1) * TILE]
            copy = pltpu.make_async_copy(both.at[m, rows, :], out.at[m, rows, :], sem.at[quarter, m])
            copy.start()
            copies.append(copy)
    for copy in copies:
        copy.wait()


def on_device(control, ensemble, obs_index, obs_value, obs_weight):
    vmem, dma = pltpu.VMEM, pltpu.SemaphoreType.DMA
    square = (TILE, TILE)
    packed = (128, 128)
    field, side_a, side_b = pl.pallas_call(
        kernel,
        out_shape=[vmem((2,) + square, f32), vmem((32, TILE), bf16), vmem((32, 2 * TILE), bf16)],
        in_specs=[pl.BlockSpec(memory_space=pltpu.HBM)] * 5,
        out_specs=[pl.BlockSpec(memory_space=vmem)] * 3,
        scratch_shapes=[
            vmem((2,) + square, f32), vmem((2,) + square, bf16),
            vmem((OBS, TILE), i32), vmem((OBS, TILE), f32), vmem((OBS, TILE), f32),
            vmem(square, bf16), vmem(square, bf16), vmem((2,) + square, bf16), vmem((2,) + square, bf16),
            vmem((2,) + square, f32), vmem(square, f32), vmem(packed, i32), vmem(square, i32),
            vmem((LEVELS,) + packed, i32),
            vmem((2, 8, 384), f32), vmem((2, len(LINES), 8, 384), f32), vmem((2, len(CORNERS), 8, 128), f32),
            vmem(packed, f32), vmem((2, RING, ROWS, 128), f32), vmem((2, ROWS, 128), f32), vmem((2,) + packed, f32),
            vmem(packed, f32), vmem(packed, f32),
            dma((6,)), dma((2,)), dma((2,)), dma((2,)), dma((2,)), dma, dma((2,)), dma((2,)), dma,
            pltpu.SemaphoreType.REGULAR, pltpu.SemaphoreType.REGULAR,
            pltpu.SemaphoreType.REGULAR, pltpu.SemaphoreType.REGULAR,
        ],
        compiler_params=pltpu.CompilerParams(
            collective_id=0, has_side_effects=True, vmem_limit_bytes=24 << 20
        ),
    )(*(
        pltpu.with_memory_space_constraint(x, pltpu.HBM)
        for x in (control, ensemble, obs_index.T, obs_value.T, obs_weight.T)
    ))
    return pl.pallas_call(
        join,
        out_shape=jax.ShapeDtypeStruct((2,) + square, f32),
        in_specs=[pl.BlockSpec(memory_space=vmem)] * 3,
        out_specs=pl.BlockSpec(memory_space=pl.ANY),
        scratch_shapes=[vmem((2,) + square, f32), dma((4, 2))],
        compiler_params=pltpu.CompilerParams(vmem_limit_bytes=8 << 20),
    )(field, side_a, side_b)


def solution(mesh):
    return jax.shard_map(
        on_device,
        mesh=mesh,
        in_specs=(
            P("mem", "gx", "gy"),
            P("mem", "gx", "gy"),
            P("gx", "gy"),
            P("gx", "gy"),
            P("gx", "gy"),
        ),
        out_specs=P("mem", "gx", "gy"),
        check_vma=False,
    )
```

```python
import functools
import math

import jax
import jax.numpy as jnp
from jax import lax
from jax.experimental import pallas as pl
from jax.experimental.pallas import tpu as pltpu
from jax.sharding import PartitionSpec as P

LEN = 400
TILE = 256
GRID = 4
RING = 16
NX = GRID * TILE
OBS = 64
saturation = 1.5
MESH = pl.DeviceIdType.MESH
f32 = jnp.float32
bf16 = jnp.bfloat16
i32 = jnp.int32
FAR = 1 << 20

CORNERS = [(dx, dy) for dy in (2, 1, 3) for dx in (2, 3, 1)]
LINES = [(0, 2), (0, 1), (0, 3), (2, 0), (3, 0), (1, 0)]
COLUMN = [8, -7, 7, -6, 6, -5, 5, -4, 4, -3, 3, -2, 2, -1, 1]
BACK = [(dz, dx) for dz in (-4, -3, 3, -2, 2, -1, 1, 0) for dx in (1, 0)][:-1]
NEAR = [(-3, 0), (3, 0), (-2, 0), (2, 0), (0, 1), (-1, 0), (1, 0)]
PIECES = 8
ROWS = 16
LEVELS = 6
HALVES = [slice(0, 128), slice(128, 256)]


def pair_scale():
    decay_rate = math.exp(-1.0 / LEN)
    return (1.0 - decay_rate * decay_rate) / (1.0 + decay_rate * decay_rate)


def decay(steps):
    return jnp.exp(steps.astype(f32) * (-1.0 / LEN))


def split(x):
    high = x.astype(bf16)
    return high, (x - high.astype(f32)).astype(bf16)


def dot(a, b, left=1, right=0):
    return lax.dot_general(a, b, (((left,), (right,)), ((), ())), preferred_element_type=f32)


def take(x, lanes):
    return jnp.take_along_axis(x, lanes, axis=1, mode="promise_in_bounds")


def iota(shape, dim):
    return lax.broadcasted_iota(i32, shape, dim)


def in_plane(dx, dy):
    return {
        "gx": lax.rem(lax.axis_index("gx") + dx, GRID),
        "gy": lax.rem(lax.axis_index("gy") + dy, GRID),
    }


def in_mem(dz, dx):
    mem = lax.axis_index("mem")
    z, half = lax.rem(mem, RING), mem // RING
    return {"mem": lax.rem(half + dx, 2) * RING + lax.rem(z + dz + RING, RING)}


def piece_of(dz):
    piece = lax.rem(lax.axis_index("mem") + dz + RING, PIECES)
    return pl.ds(pl.multiple_of(piece * ROWS, ROWS), ROWS)


def send(src, dst, send_sem, recv_sem, peer):
    pltpu.make_async_remote_copy(
        src, dst, send_sem, recv_sem, device_id=peer, device_id_type=MESH
    ).start()


def arrived(ref, sem):
    pltpu.make_async_copy(ref, ref, sem).wait()


def coefficients(axis, d, even, shape):
    me = lax.axis_index(axis)
    it = lax.rem(me - d + GRID, GRID)
    before = jnp.where(it < me, TILE * (me - it - 1) + 1, FAR)
    after = jnp.where(it > me, TILE * (it - me - 1) + 1, FAR)
    ends = 2 * NX - TILE * (me + it + 2) + 2
    own = decay(jnp.where(even, before, after))
    above = jnp.where(even, 0.0, -decay(jnp.full(shape, ends, i32)))
    return own, above


def kernel(
    control, ensemble, obs_index, obs_value, obs_weight, field, side_a, side_b,
    ctl, ens, idx, val, wgt, thi, tlo, vhi, vlo, w0, idxp, first, nexts, fcol, bcol,
    msg, lines, corners, pkb, gat, tot, res, valp, wgtp, at_ref,
    load_sem, line_send, line_recv, corner_send, corner_recv, sum_send, sum_recv, back_send, back_recv,
    near_in, column_in, other_in,
):
    loads = [
        pltpu.make_async_copy(control.at[m, rows, :], ctl.at[m, rows, :], load_sem.at[2 * m + n])
        for m in range(2)
        for n, rows in enumerate(HALVES)
    ]
    loads += [
        pltpu.make_async_copy(obs_index, idx, load_sem.at[4]),
        pltpu.make_async_copy(ensemble, ens, load_sem.at[5]),
        pltpu.make_async_copy(obs_value, val, load_sem.at[6]),
        pltpu.make_async_copy(obs_weight, wgt, load_sem.at[7]),
    ]
    for copy in loads:
        copy.start()
    barrier = pltpu.get_barrier_semaphore()
    peers = [in_mem(*o) for o in NEAR] + [in_plane(*o) for o in CORNERS + LINES]

    def signal(sem, peer):
        pl.semaphore_signal(sem, 1, device_id=peer, device_id_type=MESH)

    for peer in peers:
        signal(barrier, peer)
    mirror = 1 - 2 * lax.rem(lax.axis_index("gx"), 2)
    half = lax.axis_index("mem") // RING

    own = piece_of(0)
    square = (TILE, TILE)
    table = decay(jnp.abs(iota(square, 0) - iota(square, 1)))
    high, low = split(table)
    thi[...] = high
    tlo[...] = low
    wide = (8, TILE)
    row, column = iota(wide, 0), iota(wide, 1)
    even = (row & 1) == 0
    ends = decay(jnp.where(even, TILE - 1 - column, column))
    starts = decay(jnp.where(even, column, TILE - 1 - column))
    f_row, b_row = ends[0:1], ends[1:2]
    ends_hi = ends.astype(bf16).astype(f32)
    ends16 = jnp.concatenate([ends_hi, ends - ends_hi], axis=0).astype(bf16)
    narrow = (8, 128)
    lane = iota(narrow, 1)
    left = lane < 64
    cx = [coefficients("gx", d, even, wide) for d in range(GRID)]
    cy = [coefficients("gy", d, even, wide) for d in range(GRID)]
    cl = [coefficients("gy", d, left, narrow) for d in range(GRID)]

    down = iota((TILE, 128), 0)
    fcol[...] = decay(TILE - 1 - down)
    bcol[...] = decay(down)

    def fold(x):
        return x[0:8] + x[8:16]

    def line_sums(v, rows):
        return [jnp.sum((v * col[rows, :]).reshape(-1, 8, 128), axis=0) for col in (fcol, bcol)]

    def summarize(turn, over_x):
        x = 0.0
        for m in range(2):
            y = fold(dot(ends16, vhi[m], 1, 1) + dot(ends16, vlo[m], 1, 1))
            x = jnp.where((row >> 1) == 2 + m, y, x)
            for end in range(2):
                line = jnp.concatenate([over_x[m][side][end] for side in range(2)], axis=1)
                x = jnp.where(row == 2 * m + end, jnp.sum(line, axis=0, keepdims=True), x)
        x_hi = x.astype(bf16).astype(f32)
        x16 = jnp.concatenate([x_hi, x - x_hi], axis=0).astype(bf16)
        corner_f = jnp.sum(x * f_row, axis=1, keepdims=True)
        corner_b = jnp.sum(x * b_row, axis=1, keepdims=True)
        msg[turn, :, 0:TILE] = fold(dot(x16, thi[...]) + dot(x16, tlo[...]))
        msg[turn, :, TILE:] = jnp.where(left, corner_f, corner_b)

    def share(turn):
        for n, o in enumerate(CORNERS):
            send(
                msg.at[turn, :, pl.ds(TILE, 128)], corners.at[turn, n],
                corner_send.at[turn], corner_recv.at[turn], in_plane(*o),
            )
        for n, o in enumerate(LINES):
            send(msg.at[turn], lines.at[turn, n], line_send.at[turn], line_recv.at[turn], in_plane(*o))

    def local(m):
        u = dot(thi[...], vhi[m]) + dot(tlo[...], vhi[m]) + dot(thi[...], vlo[m])
        uhi, ulo = split(u)
        return dot(uhi, thi[...]) + dot(ulo, thi[...]) + dot(uhi, tlo[...])

    def remote(turn):
        arrived(corners.at[turn], corner_recv.at[turn])
        arrived(lines.at[turn], line_recv.at[turn])

        def block(dx, dy):
            if (dx, dy) == (0, 0):
                return msg[turn]
            return lines[turn, LINES.index((dx, dy))]

        def weigh(c, x):
            return c[0] * x + c[1] * pltpu.roll(x, 1, 0)

        xs, ys, corner = 0.0, 0.0, 0.0
        for d in range(GRID):
            xs = xs + weigh(cx[d], block(d, 0)[:, 0:TILE])
            ys = ys + weigh(cy[d], block(0, d)[:, 0:TILE])
        for dy in range(GRID):
            over_x = 0.0
            for dx in range(GRID):
                if dx and dy:
                    g = corners[turn, CORNERS.index((dx, dy))]
                else:
                    g = block(dx, dy)[:, TILE:]
                over_x = over_x + weigh((cx[dx][0][:, 0:128], cx[dx][1][:, 0:128]), g)
            corner = corner + cl[dy][0] * over_x + cl[dy][1] * pltpu.roll(over_x, 64, 1)
        ab = jnp.where(row < 4, xs + corner[:, 0:1] * b_row + corner[:, 64:65] * f_row, ys)
        a = jnp.where(row < 4, starts, ab)
        b = jnp.where(row < 4, ab, starts)
        b = jnp.concatenate([jnp.where((row & 2) == 0, b, 0.0), jnp.where((row & 2) == 0, 0.0, b)], axis=1)
        a_hi, b_hi = a.astype(bf16).astype(f32), b.astype(bf16).astype(f32)
        a_lo, b_lo = a - a_hi, b - b_hi
        a = jnp.concatenate([a_hi, a_hi, a_lo, a_lo], axis=0).astype(bf16)
        b = jnp.concatenate([b_hi, b_lo, b_hi, b_lo], axis=0).astype(bf16)
        return a, b

    def pack(ref):
        return jnp.concatenate([ref[:, 0:128], ref[:, 128:256]], axis=0).T

    over_x = [[[0.0, 0.0] for side in range(2)] for m in range(2)]

    def add_sums(m, side, v, rows):
        over_x[m][side] = [old + new for old, new in zip(over_x[m][side], line_sums(v, rows))]

    for m in range(2):
        for n, rows in enumerate(HALVES):
            loads[2 * m + n].wait()
            high, low = split(ctl[m, rows, :])
            vhi[m, rows, :] = high
            vlo[m, rows, :] = low
            for side, lanes in enumerate(HALVES):
                add_sums(m, side, ctl[m, rows, lanes], rows)
    summarize(0, over_x)
    pl.semaphore_wait(barrier, len(peers))
    for dz in (-3, 3):
        signal(near_in, in_mem(dz, 0))
    share(0)
    for m in range(2):
        w0[m] = local(m)
    loads[4].wait()
    idxp[...] = pack(idx)
    loads[5].wait()
    pl.semaphore_wait(near_in, 2)
    for dz in (-2, 2):
        signal(column_in, in_mem(dz, 0))
    a, b = remote(0)
    at_ref[...] = a.T
    for k in range(4):
        fields = []
        for above in range(2):
            rows = slice(above * 128 + k * 32, above * 128 + k * 32 + 32)
            update = dot(at_ref[rows, :], b)
            fields.append(
                ens[0, rows, :].astype(f32) * (w0[0, rows, :] + update[:, 0:TILE])
                + ens[1, rows, :].astype(f32) * (w0[1, rows, :] + update[:, TILE:])
            )
        for n in range(0, 32, 8):
            rows = slice(n, n + 8)
            at = idxp[k * 32 + n : k * 32 + n + 8, :]
            low = at & 127
            upper = at >= 128
            picked = [jnp.where(upper, take(v[rows, 128:256], low), take(v[rows, 0:128], low)) for v in fields]
            pkb[k * 32 + n : k * 32 + n + 8, :] = jnp.where(left, *picked)

    pl.semaphore_wait(column_in, 2)
    signal(other_in, in_mem(0, 1))
    for n, dz in enumerate(COLUMN):
        send(pkb.at[piece_of(dz)], gat.at[n], sum_send, sum_recv, in_mem(dz, 0))

    def find(k, carry):
        rows = pl.ds(pl.multiple_of((k // 2) * 128, 128), 128)
        lanes = pl.ds(pl.multiple_of((k % 2) * 128, 128), 128)
        cell = iota((128, 128), 0) + (k % 2) * 128
        found = jnp.full((128, 128), -1, i32)
        for j in range(OBS):
            found = jnp.where(idx[j : j + 1, rows] == cell, (k // 2) * OBS + j, found)
        first[rows, lanes] = found.T
        return carry

    lax.fori_loop(0, 4, find, 0)
    level = iota(narrow, 0)
    link = []
    for side in range(2):
        at = [idx[8 * t : 8 * t + 8, side * 128 : side * 128 + 128] for t in range(8)]
        found = [jnp.full(narrow, -1, i32) for t in range(8)]
        for j in range(OBS):
            here = at[j // 8][j % 8 : j % 8 + 1]
            for t in range(j // 8, 8):
                hit = at[t] == here
                if t == j // 8:
                    hit = hit & (level > j % 8)
                found[t] = jnp.where(hit, side * OBS + j, found[t])
        link += found
    link = jnp.concatenate(link, axis=0).T
    for n in range(LEVELS):
        nexts[n] = link
        link = jnp.where(link >= 0, take(link, jnp.maximum(link, 0)), -1)
    loads[6].wait()
    loads[7].wait()
    valp[...] = pack(val) * (1.0 / saturation)
    wgtp[...] = pack(wgt) * (saturation * pair_scale())
    pl.semaphore_wait(other_in, 1)
    arrived(gat, sum_recv)
    tot[...] = pkb[own, :] + jnp.sum(gat[...], axis=0)
    for dz, dx in BACK:
        send(tot, res.at[half, own], back_send, back_recv, in_mem(dz * mirror, dx))
    res[half, own, :] = tot[...]
    arrived(gat, back_recv)

    total = res[0] + res[1]
    residual = wgtp[...] * jnp.tanh(total * (pair_scale() / saturation) - valp[...])
    for n in range(LEVELS):
        link = nexts[n]
        residual = residual + jnp.where(link >= 0, take(residual, jnp.maximum(link, 0)), 0.0)
    over_x = [[[0.0, 0.0] for side in range(2)] for m in range(2)]
    for k in range(8):
        given = residual[k * 16 : k * 16 + 16]
        for above in range(2):
            rows = slice(above * 128 + k * 16, above * 128 + k * 16 + 16)
            for side, lanes in enumerate(HALVES):
                at = first[rows, lanes]
                forcing = jnp.where(at >= 0, take(given, jnp.maximum(at, 0)), 0.0)
                for m in range(2):
                    v = ens[m, rows, lanes].astype(f32) * forcing
                    high, low = split(v)
                    vhi[m, rows, lanes] = high
                    vlo[m, rows, lanes] = low
                    over_x[m][side] = [old + new for old, new in zip(over_x[m][side], line_sums(v, rows))]
    summarize(1, over_x)
    share(1)
    for m in range(2):
        field[m] = ctl[m] + local(m)
    arrived(gat, sum_send)
    arrived(gat, back_send)
    for turn in range(2):
        arrived(corners.at[turn], corner_send.at[turn])
        arrived(lines.at[turn], line_send.at[turn])
    a, b = remote(1)
    side_a[...] = a
    side_b[...] = b


def join(field, side_a, side_b, out, both, sem):
    copies = []
    for quarter in range(4):
        rows = slice(quarter * 64, quarter * 64 + 64)
        update = dot(side_a[:, rows], side_b[...], 0, 0)
        for m in range(2):
            both[m, rows, :] = field[m, rows, :] + update[:, m * TILE : (m + 1) * TILE]
            copy = pltpu.make_async_copy(both.at[m, rows, :], out.at[m, rows, :], sem.at[quarter, m])
            copy.start()
            copies.append(copy)
    for copy in copies:
        copy.wait()


def on_device(control, ensemble, obs_index, obs_value, obs_weight):
    vmem, dma = pltpu.VMEM, pltpu.SemaphoreType.DMA
    square = (TILE, TILE)
    packed = (128, 128)
    field, side_a, side_b = pl.pallas_call(
        kernel,
        out_shape=[vmem((2,) + square, f32), vmem((32, TILE), bf16), vmem((32, 2 * TILE), bf16)],
        in_specs=[pl.BlockSpec(memory_space=pltpu.HBM)] * 5,
        out_specs=[pl.BlockSpec(memory_space=vmem)] * 3,
        scratch_shapes=[
            vmem((2,) + square, f32), vmem((2,) + square, bf16),
            vmem((OBS, TILE), i32), vmem((OBS, TILE), f32), vmem((OBS, TILE), f32),
            vmem(square, bf16), vmem(square, bf16), vmem((2,) + square, bf16), vmem((2,) + square, bf16),
            vmem((2,) + square, f32), vmem(packed, i32), vmem(square, i32),
            vmem((LEVELS,) + packed, i32), vmem((TILE, 128), f32), vmem((TILE, 128), f32),
            vmem((2, 8, 384), f32), vmem((2, len(LINES), 8, 384), f32), vmem((2, len(CORNERS), 8, 128), f32),
            vmem(packed, f32), vmem((len(COLUMN), ROWS, 128), f32), vmem((ROWS, 128), f32), vmem((2,) + packed, f32),
            vmem(packed, f32), vmem(packed, f32), vmem((TILE, 32), bf16),
            dma((8,)), dma((2,)), dma((2,)), dma((2,)), dma((2,)), dma, dma, dma, dma,
            pltpu.SemaphoreType.REGULAR, pltpu.SemaphoreType.REGULAR, pltpu.SemaphoreType.REGULAR,
        ],
        compiler_params=pltpu.CompilerParams(
            collective_id=0, has_side_effects=True, vmem_limit_bytes=24 << 20
        ),
    )(*(
        pltpu.with_memory_space_constraint(x, pltpu.HBM)
        for x in (control, ensemble, obs_index.T, obs_value.T, obs_weight.T)
    ))
    return pl.pallas_call(
        join,
        out_shape=jax.ShapeDtypeStruct((2,) + square, f32),
        in_specs=[pl.BlockSpec(memory_space=vmem)] * 3,
        out_specs=pl.BlockSpec(memory_space=pl.ANY),
        scratch_shapes=[vmem((2,) + square, f32), dma((4, 2))],
        compiler_params=pltpu.CompilerParams(vmem_limit_bytes=8 << 20),
    )(field, side_a, side_b)


def solution(mesh):
    return jax.shard_map(
        on_device,
        mesh=mesh,
        in_specs=(
            P("mem", "gx", "gy"),
            P("mem", "gx", "gy"),
            P("gx", "gy"),
            P("gx", "gy"),
            P("gx", "gy"),
        ),
        out_specs=P("mem", "gx", "gy"),
        check_vma=False,
    )
```

```python
import functools
import math

import jax
import jax.numpy as jnp
from jax import lax
from jax.experimental import pallas as pl
from jax.experimental.pallas import tpu as pltpu
from jax.sharding import PartitionSpec as P

LEN = 400
TILE = 256
GRID = 4
RING = 16
NX = GRID * TILE
OBS = 64
saturation = 1.5
MESH = pl.DeviceIdType.MESH
f32 = jnp.float32
bf16 = jnp.bfloat16
i32 = jnp.int32
FAR = 1 << 20

CORNERS = [(dx, dy) for dy in (2, 1, 3) for dx in (2, 3, 1)]
LINES = [(0, 2), (0, 1), (0, 3), (2, 0), (3, 0), (1, 0)]
COLUMN = [8, -7, 7, -6, 6, -5, 5, -4, 4, -3, 3, -2, 2, -1, 1]
AROUND = [(dz, dx) for dz in COLUMN + [0] for dx in (1, 0)][:-1]
WINDOW = [(dz, dx) for dz in (-4, -3, 3, -2, 2, -1, 1, 0) for dx in (1, 0)][:-1]
NEAR = [(-3, 0), (3, 0), (-2, 0), (2, 0), (0, 1), (-1, 0), (1, 0)]
PIECES = 8
WIDE = 16
THIN = 8
LEVELS = 6
HALVES = [slice(0, 128), slice(128, 256)]


def pair_scale():
    decay_rate = math.exp(-1.0 / LEN)
    return (1.0 - decay_rate * decay_rate) / (1.0 + decay_rate * decay_rate)


def decay(steps):
    return jnp.exp(steps.astype(f32) * (-1.0 / LEN))


def split(x):
    high = x.astype(bf16)
    return high, (x - high.astype(f32)).astype(bf16)


def dot(a, b, left=1, right=0):
    return lax.dot_general(a, b, (((left,), (right,)), ((), ())), preferred_element_type=f32)


def take(x, lanes):
    return jnp.take_along_axis(x, lanes, axis=1, mode="promise_in_bounds")


def iota(shape, dim):
    return lax.broadcasted_iota(i32, shape, dim)


def in_plane(dx, dy):
    return {
        "gx": lax.rem(lax.axis_index("gx") + dx, GRID),
        "gy": lax.rem(lax.axis_index("gy") + dy, GRID),
    }


def in_mem(dz, dx):
    mem = lax.axis_index("mem")
    z, half = lax.rem(mem, RING), mem // RING
    return {"mem": lax.rem(half + dx, 2) * RING + lax.rem(z + dz + RING, RING)}


def wide_piece(dz):
    piece = lax.rem(lax.axis_index("mem") + dz + RING, PIECES)
    return pl.ds(pl.multiple_of(piece * WIDE, WIDE), WIDE)


def thin_piece(dz, dx):
    mem = lax.axis_index("mem")
    piece = lax.rem(mem + dz + RING, PIECES) * 2 + lax.rem(mem // RING + dx, 2)
    return pl.ds(pl.multiple_of(piece * THIN, THIN), THIN)


def send(src, dst, send_sem, recv_sem, peer):
    pltpu.make_async_remote_copy(
        src, dst, send_sem, recv_sem, device_id=peer, device_id_type=MESH
    ).start()


def arrived(ref, sem):
    pltpu.make_async_copy(ref, ref, sem).wait()


def coefficients(axis, d, even, shape):
    me = lax.axis_index(axis)
    it = lax.rem(me - d + GRID, GRID)
    before = jnp.where(it < me, TILE * (me - it - 1) + 1, FAR)
    after = jnp.where(it > me, TILE * (it - me - 1) + 1, FAR)
    ends = 2 * NX - TILE * (me + it + 2) + 2
    own = decay(jnp.where(even, before, after))
    above = jnp.where(even, 0.0, -decay(jnp.full(shape, ends, i32)))
    return own, above


def kernel(
    control, ensemble, obs_index, obs_value, obs_weight, field, side_a, side_b,
    ctl, ens, idx, val, wgt, thi, tlo, vhi, vlo, w0, idxp, first, nexts, fcol, bcol,
    msg, lines, corners, pkb, gat, thin, tot, res, valp, wgtp, at_ref,
    load_sem, line_send, line_recv, corner_send, corner_recv, sum_send, sum_recv, back_send, back_recv,
    near_in, column_in, other_in, all_in,
):
    loads = [
        pltpu.make_async_copy(control.at[m, rows, :], ctl.at[m, rows, :], load_sem.at[2 * m + n])
        for m in range(2)
        for n, rows in enumerate(HALVES)
    ]
    loads += [
        pltpu.make_async_copy(obs_index, idx, load_sem.at[4]),
        pltpu.make_async_copy(ensemble, ens, load_sem.at[5]),
        pltpu.make_async_copy(obs_value, val, load_sem.at[6]),
        pltpu.make_async_copy(obs_weight, wgt, load_sem.at[7]),
    ]
    for copy in loads:
        copy.start()
    barrier = pltpu.get_barrier_semaphore()
    peers = [in_plane(*o) for o in CORNERS] + [in_mem(*o) for o in NEAR] + [in_plane(*o) for o in LINES]

    def signal(sem, peer):
        pl.semaphore_signal(sem, 1, device_id=peer, device_id_type=MESH)

    for peer in peers:
        signal(barrier, peer)
    core = lax.rem(lax.axis_index("gx"), 2)
    mem = lax.axis_index("mem")
    half, turned = mem // RING, lax.rem(mem, RING) // PIECES

    wide_own, thin_own = wide_piece(0), thin_piece(0, 0)
    square = (TILE, TILE)
    table = decay(jnp.abs(iota(square, 0) - iota(square, 1)))
    high, low = split(table)
    thi[...] = high
    tlo[...] = low
    wide = (8, TILE)
    row, column = iota(wide, 0), iota(wide, 1)
    even = (row & 1) == 0
    ends = decay(jnp.where(even, TILE - 1 - column, column))
    starts = decay(jnp.where(even, column, TILE - 1 - column))
    f_row, b_row = ends[0:1], ends[1:2]
    ends_hi = ends.astype(bf16).astype(f32)
    ends16 = jnp.concatenate([ends_hi, ends - ends_hi], axis=0).astype(bf16)
    narrow = (8, 128)
    lane = iota(narrow, 1)
    left = lane < 64
    cx = [coefficients("gx", d, even, wide) for d in range(GRID)]
    cy = [coefficients("gy", d, even, wide) for d in range(GRID)]
    cl = [coefficients("gy", d, left, narrow) for d in range(GRID)]

    down = iota((TILE, 128), 0)
    fcol[...] = decay(TILE - 1 - down)
    bcol[...] = decay(down)

    def fold(x):
        return x[0:8] + x[8:16]

    def line_sums(v, rows):
        return [jnp.sum((v * col[rows, :]).reshape(-1, 8, 128), axis=0) for col in (fcol, bcol)]

    def summarize(turn, over_x):
        x = 0.0
        for m in range(2):
            y = fold(dot(ends16, vhi[m], 1, 1) + dot(ends16, vlo[m], 1, 1))
            x = jnp.where((row >> 1) == 2 + m, y, x)
            for end in range(2):
                line = jnp.concatenate([over_x[m][side][end] for side in range(2)], axis=1)
                x = jnp.where(row == 2 * m + end, jnp.sum(line, axis=0, keepdims=True), x)
        x_hi = x.astype(bf16).astype(f32)
        x16 = jnp.concatenate([x_hi, x - x_hi], axis=0).astype(bf16)
        corner_f = jnp.sum(x * f_row, axis=1, keepdims=True)
        corner_b = jnp.sum(x * b_row, axis=1, keepdims=True)
        msg[turn, :, 0:TILE] = fold(dot(x16, thi[...]) + dot(x16, tlo[...]))
        msg[turn, :, TILE:] = jnp.where(left, corner_f, corner_b)

    def share(turn):
        for n, o in enumerate(CORNERS):
            send(
                msg.at[turn, :, pl.ds(TILE, 128)], corners.at[turn, n],
                corner_send.at[turn], corner_recv.at[turn], in_plane(*o),
            )
        for n, o in enumerate(LINES):
            send(msg.at[turn], lines.at[turn, n], line_send.at[turn], line_recv.at[turn], in_plane(*o))

    def local(m):
        u = dot(thi[...], vhi[m]) + dot(tlo[...], vhi[m]) + dot(thi[...], vlo[m])
        uhi, ulo = split(u)
        return dot(uhi, thi[...]) + dot(ulo, thi[...]) + dot(uhi, tlo[...])

    def remote(turn):
        arrived(corners.at[turn], corner_recv.at[turn])
        arrived(lines.at[turn], line_recv.at[turn])

        def block(dx, dy):
            if (dx, dy) == (0, 0):
                return msg[turn]
            return lines[turn, LINES.index((dx, dy))]

        def weigh(c, x):
            return c[0] * x + c[1] * pltpu.roll(x, 1, 0)

        xs, ys, corner = 0.0, 0.0, 0.0
        for d in range(GRID):
            xs = xs + weigh(cx[d], block(d, 0)[:, 0:TILE])
            ys = ys + weigh(cy[d], block(0, d)[:, 0:TILE])
        for dy in range(GRID):
            over_x = 0.0
            for dx in range(GRID):
                if dx and dy:
                    g = corners[turn, CORNERS.index((dx, dy))]
                else:
                    g = block(dx, dy)[:, TILE:]
                over_x = over_x + weigh((cx[dx][0][:, 0:128], cx[dx][1][:, 0:128]), g)
            corner = corner + cl[dy][0] * over_x + cl[dy][1] * pltpu.roll(over_x, 64, 1)
        ab = jnp.where(row < 4, xs + corner[:, 0:1] * b_row + corner[:, 64:65] * f_row, ys)
        a = jnp.where(row < 4, starts, ab)
        b = jnp.where(row < 4, ab, starts)
        b = jnp.concatenate([jnp.where((row & 2) == 0, b, 0.0), jnp.where((row & 2) == 0, 0.0, b)], axis=1)
        a_hi, b_hi = a.astype(bf16).astype(f32), b.astype(bf16).astype(f32)
        a_lo, b_lo = a - a_hi, b - b_hi
        a = jnp.concatenate([a_hi, a_hi, a_lo, a_lo], axis=0).astype(bf16)
        b = jnp.concatenate([b_hi, b_lo, b_hi, b_lo], axis=0).astype(bf16)
        return a, b

    def pack(ref):
        return jnp.concatenate([ref[:, 0:128], ref[:, 128:256]], axis=0).T

    over_x = [[[0.0, 0.0] for side in range(2)] for m in range(2)]

    def add_sums(m, side, v, rows):
        over_x[m][side] = [old + new for old, new in zip(over_x[m][side], line_sums(v, rows))]

    for m in range(2):
        for n, rows in enumerate(HALVES):
            loads[2 * m + n].wait()
            high, low = split(ctl[m, rows, :])
            vhi[m, rows, :] = high
            vlo[m, rows, :] = low
            for side, lanes in enumerate(HALVES):
                add_sums(m, side, ctl[m, rows, lanes], rows)
    summarize(0, over_x)
    pl.semaphore_wait(barrier, len(peers))
    for dz in (-3, 3):
        signal(near_in, in_mem(dz, 0))
    share(0)
    for m in range(2):
        w0[m] = local(m)
    loads[4].wait()
    idxp[...] = pack(idx)
    loads[5].wait()
    pl.semaphore_wait(near_in, 2)
    for dz in (-2, 2):
        signal(column_in, in_mem(dz, 0))
    signal(other_in, in_mem(0, 1))
    a, b = remote(0)
    at_ref[...] = a.T
    for k in range(4):
        fields = []
        for above in range(2):
            rows = slice(above * 128 + k * 32, above * 128 + k * 32 + 32)
            update = dot(at_ref[rows, :], b)
            fields.append(
                ens[0, rows, :].astype(f32) * (w0[0, rows, :] + update[:, 0:TILE])
                + ens[1, rows, :].astype(f32) * (w0[1, rows, :] + update[:, TILE:])
            )
        for n in range(0, 32, 8):
            rows = slice(n, n + 8)
            at = idxp[k * 32 + n : k * 32 + n + 8, :]
            low = at & 127
            upper = at >= 128
            picked = [jnp.where(upper, take(v[rows, 128:256], low), take(v[rows, 0:128], low)) for v in fields]
            pkb[k * 32 + n : k * 32 + n + 8, :] = jnp.where(left, *picked)

    pl.semaphore_wait(column_in, 2)
    pl.semaphore_wait(other_in, 1)
    signal(all_in, in_mem(0, 1))

    @pl.when(core == 0)
    def _():
        for n, dz in enumerate(COLUMN):
            send(pkb.at[wide_piece(dz)], gat.at[n], sum_send, sum_recv, in_mem(dz, 0))

    @pl.when(core == 1)
    def _():
        for n, o in enumerate(WINDOW):
            send(pkb.at[thin_piece(*o)], thin.at[n], sum_send, sum_recv, in_mem(*o))

    def find(k, carry):
        rows = pl.ds(pl.multiple_of((k // 2) * 128, 128), 128)
        lanes = pl.ds(pl.multiple_of((k % 2) * 128, 128), 128)
        cell = iota((128, 128), 0) + (k % 2) * 128
        found = jnp.full((128, 128), -1, i32)
        for j in range(OBS):
            found = jnp.where(idx[j : j + 1, rows] == cell, (k // 2) * OBS + j, found)
        first[rows, lanes] = found.T
        return carry

    lax.fori_loop(0, 4, find, 0)
    level = iota(narrow, 0)
    link = []
    for side in range(2):
        at = [idx[8 * t : 8 * t + 8, side * 128 : side * 128 + 128] for t in range(8)]
        found = [jnp.full(narrow, -1, i32) for t in range(8)]
        for j in range(OBS):
            here = at[j // 8][j % 8 : j % 8 + 1]
            for t in range(j // 8, 8):
                hit = at[t] == here
                if t == j // 8:
                    hit = hit & (level > j % 8)
                found[t] = jnp.where(hit, side * OBS + j, found[t])
        link += found
    link = jnp.concatenate(link, axis=0).T
    for n in range(LEVELS):
        nexts[n] = link
        link = jnp.where(link >= 0, take(link, jnp.maximum(link, 0)), -1)
    loads[6].wait()
    loads[7].wait()
    valp[...] = pack(val) * (1.0 / saturation)
    wgtp[...] = pack(wgt) * (saturation * pair_scale())
    pl.semaphore_wait(all_in, 1)

    @pl.when(core == 0)
    def _():
        arrived(gat, sum_recv)
        tot[...] = pkb[wide_own, :] + jnp.sum(gat[...], axis=0)
        for o in WINDOW:
            send(tot, res.at[half, wide_own], back_send, back_recv, in_mem(*o))
        res[half, wide_own, :] = tot[...]
        arrived(gat, back_recv)

    @pl.when(core == 1)
    def _():
        arrived(thin.at[pl.ds(0, len(WINDOW))], sum_recv)
        some = tot.at[pl.ds(0, THIN)]
        some[...] = pkb[thin_own, :] + jnp.sum(thin[0 : len(WINDOW)], axis=0)
        for o in AROUND:
            send(some, res.at[turned, thin_own], back_send, back_recv, in_mem(*o))
        res[turned, thin_own, :] = some[...]
        arrived(thin, back_recv)

    total = res[0] + res[1]
    residual = wgtp[...] * jnp.tanh(total * (pair_scale() / saturation) - valp[...])
    for n in range(LEVELS):
        link = nexts[n]
        residual = residual + jnp.where(link >= 0, take(residual, jnp.maximum(link, 0)), 0.0)
    over_x = [[[0.0, 0.0] for side in range(2)] for m in range(2)]
    for k in range(8):
        given = residual[k * 16 : k * 16 + 16]
        for above in range(2):
            rows = slice(above * 128 + k * 16, above * 128 + k * 16 + 16)
            for side, lanes in enumerate(HALVES):
                at = first[rows, lanes]
                forcing = jnp.where(at >= 0, take(given, jnp.maximum(at, 0)), 0.0)
                for m in range(2):
                    v = ens[m, rows, lanes].astype(f32) * forcing
                    high, low = split(v)
                    vhi[m, rows, lanes] = high
                    vlo[m, rows, lanes] = low
                    over_x[m][side] = [old + new for old, new in zip(over_x[m][side], line_sums(v, rows))]
    summarize(1, over_x)
    share(1)
    for m in range(2):
        field[m] = ctl[m] + local(m)
    @pl.when(core == 0)
    def _():
        arrived(gat, sum_send)
        arrived(gat, back_send)

    @pl.when(core == 1)
    def _():
        arrived(thin.at[pl.ds(0, len(WINDOW))], sum_send)
        arrived(thin, back_send)

    for turn in range(2):
        arrived(corners.at[turn], corner_send.at[turn])
        arrived(lines.at[turn], line_send.at[turn])
    a, b = remote(1)
    side_a[...] = a
    side_b[...] = b


def join(field, side_a, side_b, out, both, sem):
    copies = []
    for quarter in range(4):
        rows = slice(quarter * 64, quarter * 64 + 64)
        update = dot(side_a[:, rows], side_b[...], 0, 0)
        for m in range(2):
            both[m, rows, :] = field[m, rows, :] + update[:, m * TILE : (m + 1) * TILE]
            copy = pltpu.make_async_copy(both.at[m, rows, :], out.at[m, rows, :], sem.at[quarter, m])
            copy.start()
            copies.append(copy)
    for copy in copies:
        copy.wait()


def on_device(control, ensemble, obs_index, obs_value, obs_weight):
    vmem, dma = pltpu.VMEM, pltpu.SemaphoreType.DMA
    square = (TILE, TILE)
    packed = (128, 128)
    field, side_a, side_b = pl.pallas_call(
        kernel,
        out_shape=[vmem((2,) + square, f32), vmem((32, TILE), bf16), vmem((32, 2 * TILE), bf16)],
        in_specs=[pl.BlockSpec(memory_space=pltpu.HBM)] * 5,
        out_specs=[pl.BlockSpec(memory_space=vmem)] * 3,
        scratch_shapes=[
            vmem((2,) + square, f32), vmem((2,) + square, bf16),
            vmem((OBS, TILE), i32), vmem((OBS, TILE), f32), vmem((OBS, TILE), f32),
            vmem(square, bf16), vmem(square, bf16), vmem((2,) + square, bf16), vmem((2,) + square, bf16),
            vmem((2,) + square, f32), vmem(packed, i32), vmem(square, i32),
            vmem((LEVELS,) + packed, i32), vmem((TILE, 128), f32), vmem((TILE, 128), f32),
            vmem((2, 8, 384), f32), vmem((2, len(LINES), 8, 384), f32), vmem((2, len(CORNERS), 8, 128), f32),
            vmem(packed, f32), vmem((len(COLUMN), WIDE, 128), f32), vmem((len(AROUND), THIN, 128), f32), vmem((WIDE, 128), f32), vmem((2,) + packed, f32),
            vmem(packed, f32), vmem(packed, f32), vmem((TILE, 32), bf16),
            dma((8,)), dma((2,)), dma((2,)), dma((2,)), dma((2,)), dma, dma, dma, dma,
            pltpu.SemaphoreType.REGULAR, pltpu.SemaphoreType.REGULAR, pltpu.SemaphoreType.REGULAR, pltpu.SemaphoreType.REGULAR,
        ],
        compiler_params=pltpu.CompilerParams(
            collective_id=0, has_side_effects=True, vmem_limit_bytes=24 << 20
        ),
    )(*(
        pltpu.with_memory_space_constraint(x, pltpu.HBM)
        for x in (control, ensemble, obs_index.T, obs_value.T, obs_weight.T)
    ))
    return pl.pallas_call(
        join,
        out_shape=jax.ShapeDtypeStruct((2,) + square, f32),
        in_specs=[pl.BlockSpec(memory_space=vmem)] * 3,
        out_specs=pl.BlockSpec(memory_space=pl.ANY),
        scratch_shapes=[vmem((2,) + square, f32), dma((4, 2))],
        compiler_params=pltpu.CompilerParams(vmem_limit_bytes=8 << 20),
    )(field, side_a, side_b)


def solution(mesh):
    return jax.shard_map(
        on_device,
        mesh=mesh,
        in_specs=(
            P("mem", "gx", "gy"),
            P("mem", "gx", "gy"),
            P("gx", "gy"),
            P("gx", "gy"),
            P("gx", "gy"),
        ),
        out_specs=P("mem", "gx", "gy"),
        check_vma=False,
    )
```

```python
import functools
import math

import jax
import jax.numpy as jnp
from jax import lax
from jax.experimental import pallas as pl
from jax.experimental.pallas import tpu as pltpu
from jax.sharding import PartitionSpec as P

LEN = 400
TILE = 256
GRID = 4
RING = 16
NX = GRID * TILE
OBS = 64
saturation = 1.5
MESH = pl.DeviceIdType.MESH
f32 = jnp.float32
bf16 = jnp.bfloat16
i32 = jnp.int32
FAR = 1 << 20

CORNERS = [(dx, dy) for dy in (2, 1, 3) for dx in (2, 3, 1)]
LINES = [(0, 2), (0, 1), (0, 3), (2, 0), (3, 0), (1, 0)]
COLUMN = [8, -7, 7, -6, 6, -5, 5, -4, 4, -3, 3, -2, 2, -1, 1]
AROUND = [(dz, dx) for dz in COLUMN + [0] for dx in (1, 0)][:-1]
WINDOW = [(dz, dx) for dz in (-4, -3, 3, -2, 2, -1, 1, 0) for dx in (1, 0)][:-1]
NEAR = [(-3, 0), (3, 0), (-2, 0), (2, 0), (0, 1), (-1, 0), (1, 0)]
PIECES = 8
WIDE = 16
THIN = 8
LEVELS = 6
HALVES = [slice(0, 128), slice(128, 256)]


def pair_scale():
    decay_rate = math.exp(-1.0 / LEN)
    return (1.0 - decay_rate * decay_rate) / (1.0 + decay_rate * decay_rate)


def decay(steps):
    return jnp.exp(steps.astype(f32) * (-1.0 / LEN))


def split(x):
    high = x.astype(bf16)
    return high, (x - high.astype(f32)).astype(bf16)


def dot(a, b, left=1, right=0):
    return lax.dot_general(a, b, (((left,), (right,)), ((), ())), preferred_element_type=f32)


def take(x, lanes):
    return jnp.take_along_axis(x, lanes, axis=1, mode="promise_in_bounds")


def iota(shape, dim):
    return lax.broadcasted_iota(i32, shape, dim)


def in_plane(dx, dy):
    return {
        "gx": lax.rem(lax.axis_index("gx") + dx, GRID),
        "gy": lax.rem(lax.axis_index("gy") + dy, GRID),
    }


def in_mem(dz, dx):
    mem = lax.axis_index("mem")
    z, half = lax.rem(mem, RING), mem // RING
    return {"mem": lax.rem(half + dx, 2) * RING + lax.rem(z + dz + RING, RING)}


def wide_piece(dz):
    piece = lax.rem(lax.axis_index("mem") + dz + RING, PIECES)
    return pl.ds(pl.multiple_of(piece * WIDE, WIDE), WIDE)


def thin_piece(dz, dx):
    mem = lax.axis_index("mem")
    piece = lax.rem(mem + dz + RING, PIECES) * 2 + lax.rem(mem // RING + dx, 2)
    return pl.ds(pl.multiple_of(piece * THIN, THIN), THIN)


def send(src, dst, send_sem, recv_sem, peer):
    pltpu.make_async_remote_copy(
        src, dst, send_sem, recv_sem, device_id=peer, device_id_type=MESH
    ).start()


def arrived(ref, sem):
    pltpu.make_async_copy(ref, ref, sem).wait()


def coefficients(axis, d, even, shape):
    me = lax.axis_index(axis)
    it = lax.rem(me - d + GRID, GRID)
    before = jnp.where(it < me, TILE * (me - it - 1) + 1, FAR)
    after = jnp.where(it > me, TILE * (it - me - 1) + 1, FAR)
    ends = 2 * NX - TILE * (me + it + 2) + 2
    own = decay(jnp.where(even, before, after))
    above = jnp.where(even, 0.0, -decay(jnp.full(shape, ends, i32)))
    return own, above


def kernel(
    control, ensemble, obs_index, obs_value, obs_weight, field, side_a, side_b,
    ctl, ens, idx, val, wgt, thi, tlo, vhi, vlo, w0, idxp, perm, first, nexts, fcol, bcol,
    msg, lines, corners, pkb, gat, thin, tot, res, valp, wgtp, at_ref,
    load_sem, line_send, line_recv, corner_send, corner_recv, sum_send, sum_recv, back_send, back_recv,
    near_in, column_in, other_in, all_in,
):
    loads = [
        pltpu.make_async_copy(control.at[m, rows, :], ctl.at[m, rows, :], load_sem.at[2 * m + n])
        for m in range(2)
        for n, rows in enumerate(HALVES)
    ]
    loads += [
        pltpu.make_async_copy(obs_index, idx, load_sem.at[4]),
        pltpu.make_async_copy(ensemble, ens, load_sem.at[5]),
        pltpu.make_async_copy(obs_value, val, load_sem.at[6]),
        pltpu.make_async_copy(obs_weight, wgt, load_sem.at[7]),
    ]
    for copy in loads:
        copy.start()
    barrier = pltpu.get_barrier_semaphore()
    peers = [in_plane(*o) for o in CORNERS] + [in_mem(*o) for o in NEAR] + [in_plane(*o) for o in LINES]

    def signal(sem, peer):
        pl.semaphore_signal(sem, 1, device_id=peer, device_id_type=MESH)

    for peer in peers:
        signal(barrier, peer)
    core = lax.rem(lax.axis_index("gx"), 2)
    mem = lax.axis_index("mem")
    half, turned = mem // RING, lax.rem(mem, RING) // PIECES

    wide_own, thin_own = wide_piece(0), thin_piece(0, 0)
    square = (TILE, TILE)
    table = decay(jnp.abs(iota(square, 0) - iota(square, 1)))
    high, low = split(table)
    thi[...] = high
    tlo[...] = low
    wide = (8, TILE)
    row, column = iota(wide, 0), iota(wide, 1)
    even = (row & 1) == 0
    ends = decay(jnp.where(even, TILE - 1 - column, column))
    starts = decay(jnp.where(even, column, TILE - 1 - column))
    f_row, b_row = ends[0:1], ends[1:2]
    ends_hi = ends.astype(bf16).astype(f32)
    ends16 = jnp.concatenate([ends_hi, ends - ends_hi], axis=0).astype(bf16)
    narrow = (8, 128)
    lane = iota(narrow, 1)
    left = lane < 64
    cx = [coefficients("gx", d, even, wide) for d in range(GRID)]
    cy = [coefficients("gy", d, even, wide) for d in range(GRID)]
    cl = [coefficients("gy", d, left, narrow) for d in range(GRID)]

    down = iota((TILE, 128), 0)
    fcol[...] = decay(TILE - 1 - down)
    bcol[...] = decay(down)

    def fold(x):
        return x[0:8] + x[8:16]

    def line_sums(v, rows):
        return [jnp.sum((v * col[rows, :]).reshape(-1, 8, 128), axis=0) for col in (fcol, bcol)]

    def summarize(turn, over_x):
        x = 0.0
        for m in range(2):
            for end in range(2):
                line = jnp.concatenate([over_x[m][side][end] for side in range(2)], axis=1)
                x = jnp.where(row == 2 * m + end, jnp.sum(line, axis=0, keepdims=True), x)
        corner_f = jnp.sum(x * f_row, axis=1, keepdims=True)
        corner_b = jnp.sum(x * b_row, axis=1, keepdims=True)
        msg[turn, :, TILE:] = jnp.where(left, corner_f, corner_b)
        return x

    def complete(turn, x):
        for m in range(2):
            y = fold(dot(ends16, vhi[m], 1, 1) + dot(ends16, vlo[m], 1, 1))
            x = jnp.where((row >> 1) == 2 + m, y, x)
        x_hi = x.astype(bf16).astype(f32)
        x16 = jnp.concatenate([x_hi, x - x_hi], axis=0).astype(bf16)
        msg[turn, :, 0:TILE] = fold(dot(x16, thi[...]) + dot(x16, tlo[...]))

    def share_corners(turn):
        for n, o in enumerate(CORNERS):
            send(
                msg.at[turn, :, pl.ds(TILE, 128)], corners.at[turn, n],
                corner_send.at[turn], corner_recv.at[turn], in_plane(*o),
            )

    def share_lines(turn):
        for n, o in enumerate(LINES):
            send(msg.at[turn], lines.at[turn, n], line_send.at[turn], line_recv.at[turn], in_plane(*o))

    def local(m):
        u = dot(thi[...], vhi[m]) + dot(tlo[...], vhi[m]) + dot(thi[...], vlo[m])
        uhi, ulo = split(u)
        return dot(uhi, thi[...]) + dot(ulo, thi[...]) + dot(uhi, tlo[...])

    def remote(turn):
        arrived(corners.at[turn], corner_recv.at[turn])
        arrived(lines.at[turn], line_recv.at[turn])

        def block(dx, dy):
            if (dx, dy) == (0, 0):
                return msg[turn]
            return lines[turn, LINES.index((dx, dy))]

        def weigh(c, x):
            return c[0] * x + c[1] * pltpu.roll(x, 1, 0)

        xs, ys, corner = 0.0, 0.0, 0.0
        for d in range(GRID):
            xs = xs + weigh(cx[d], block(d, 0)[:, 0:TILE])
            ys = ys + weigh(cy[d], block(0, d)[:, 0:TILE])
        for dy in range(GRID):
            over_x = 0.0
            for dx in range(GRID):
                if dx and dy:
                    g = corners[turn, CORNERS.index((dx, dy))]
                else:
                    g = block(dx, dy)[:, TILE:]
                over_x = over_x + weigh((cx[dx][0][:, 0:128], cx[dx][1][:, 0:128]), g)
            corner = corner + cl[dy][0] * over_x + cl[dy][1] * pltpu.roll(over_x, 64, 1)
        ab = jnp.where(row < 4, xs + corner[:, 0:1] * b_row + corner[:, 64:65] * f_row, ys)
        a = jnp.where(row < 4, starts, ab)
        b = jnp.where(row < 4, ab, starts)
        b = jnp.concatenate([jnp.where((row & 2) == 0, b, 0.0), jnp.where((row & 2) == 0, 0.0, b)], axis=1)
        a_hi, b_hi = a.astype(bf16).astype(f32), b.astype(bf16).astype(f32)
        a_lo, b_lo = a - a_hi, b - b_hi
        a = jnp.concatenate([a_hi, a_hi, a_lo, a_lo], axis=0).astype(bf16)
        b = jnp.concatenate([b_hi, b_lo, b_hi, b_lo], axis=0).astype(bf16)
        return a, b

    def pack(ref):
        return jnp.concatenate([ref[:, 0:128], ref[:, 128:256]], axis=0).T

    over_x = [[[0.0, 0.0] for side in range(2)] for m in range(2)]

    def add_sums(m, side, v, rows):
        over_x[m][side] = [old + new for old, new in zip(over_x[m][side], line_sums(v, rows))]

    for m in range(2):
        for n, rows in enumerate(HALVES):
            loads[2 * m + n].wait()
            high, low = split(ctl[m, rows, :])
            vhi[m, rows, :] = high
            vlo[m, rows, :] = low
            for side, lanes in enumerate(HALVES):
                add_sums(m, side, ctl[m, rows, lanes], rows)
    complete(0, summarize(0, over_x))
    pl.semaphore_wait(barrier, len(peers))
    for dz in (-3, 3):
        signal(near_in, in_mem(dz, 0))
    share_corners(0)
    share_lines(0)
    for m in range(2):
        w0[m] = local(m)
    loads[4].wait()
    level = iota(narrow, 0)
    order = []
    for side in range(2):
        at = [idx[8 * t : 8 * t + 8, side * 128 : side * 128 + 128] for t in range(8)]
        rank = [jnp.zeros(narrow, i32) for t in range(8)]
        for j in range(OBS):
            here = at[j // 8][j % 8 : j % 8 + 1]
            for t in range(8):
                if t < j // 8:
                    ahead = here < at[t]
                elif t > j // 8:
                    ahead = here <= at[t]
                else:
                    ahead = (here < at[t]) | ((here == at[t]) & (level > j % 8))
                rank[t] = rank[t] + jnp.where(ahead, 1, 0)
        found = [jnp.zeros(narrow, i32) for t in range(8)]
        for j in range(OBS):
            place_of = rank[j // 8][j % 8 : j % 8 + 1]
            for t in range(8):
                found[t] = jnp.where(place_of == level + 8 * t, side * OBS + j, found[t])
        order += found
    perm[...] = jnp.concatenate(order, axis=0).T
    idxp[...] = take(pack(idx), perm[...])
    loads[5].wait()
    pl.semaphore_wait(near_in, 2)
    for dz in (-2, 2):
        signal(column_in, in_mem(dz, 0))
    signal(other_in, in_mem(0, 1))
    a, b = remote(0)
    at_ref[...] = a.T
    for k in range(4):
        fields = []
        for above in range(2):
            rows = slice(above * 128 + k * 32, above * 128 + k * 32 + 32)
            update = dot(at_ref[rows, :], b)
            fields.append(
                ens[0, rows, :].astype(f32) * (w0[0, rows, :] + update[:, 0:TILE])
                + ens[1, rows, :].astype(f32) * (w0[1, rows, :] + update[:, TILE:])
            )
        for n in range(0, 32, 8):
            rows = slice(n, n + 8)
            at = idxp[k * 32 + n : k * 32 + n + 8, :]
            low = at & 127
            upper = at >= 128
            picked = [jnp.where(upper, take(v[rows, 128:256], low), take(v[rows, 0:128], low)) for v in fields]
            pkb[k * 32 + n : k * 32 + n + 8, :] = jnp.where(left, *picked)

    pl.semaphore_wait(column_in, 2)
    pl.semaphore_wait(other_in, 1)
    signal(all_in, in_mem(0, 1))

    @pl.when(core == 0)
    def _():
        for n, dz in enumerate(COLUMN):
            send(pkb.at[wide_piece(dz)], gat.at[n], sum_send, sum_recv, in_mem(dz, 0))

    @pl.when(core == 1)
    def _():
        for n, o in enumerate(WINDOW):
            send(pkb.at[thin_piece(*o)], thin.at[n], sum_send, sum_recv, in_mem(*o))

    cells = idxp[...].T
    for side in range(2):
        idx[:, side * 128 : side * 128 + 128] = cells[side * OBS : side * OBS + OBS]

    def find(k, carry):
        rows = pl.ds(pl.multiple_of((k // 2) * 128, 128), 128)
        lanes = pl.ds(pl.multiple_of((k % 2) * 128, 128), 128)
        cell = iota((128, 128), 0) + (k % 2) * 128
        found = jnp.full((128, 128), -1, i32)
        for j in range(OBS):
            found = jnp.where(idx[j : j + 1, rows] == cell, (k // 2) * OBS + j, found)
        first[rows, lanes] = found.T
        return carry

    lax.fori_loop(0, 4, find, 0)
    cells = idxp[...] + jnp.where(iota((128, 128), 1) < OBS, 0, TILE)
    for n in range(LEVELS):
        nexts[n] = jnp.where(cells == pltpu.roll(cells, 1 << n, 1), 1.0, 0.0)
    loads[6].wait()
    loads[7].wait()
    valp[...] = take(pack(val), perm[...]) * (1.0 / saturation)
    wgtp[...] = take(pack(wgt), perm[...]) * (saturation * pair_scale())
    pl.semaphore_wait(all_in, 1)

    @pl.when(core == 0)
    def _():
        arrived(gat, sum_recv)
        tot[...] = pkb[wide_own, :] + jnp.sum(gat[...], axis=0)
        for o in WINDOW:
            send(tot, res.at[half, wide_own], back_send, back_recv, in_mem(*o))
        res[half, wide_own, :] = tot[...]
        arrived(gat, back_recv)

    @pl.when(core == 1)
    def _():
        arrived(thin.at[pl.ds(0, len(WINDOW))], sum_recv)
        some = tot.at[pl.ds(0, THIN)]
        some[...] = pkb[thin_own, :] + jnp.sum(thin[0 : len(WINDOW)], axis=0)
        for o in AROUND:
            send(some, res.at[turned, thin_own], back_send, back_recv, in_mem(*o))
        res[turned, thin_own, :] = some[...]
        arrived(thin, back_recv)

    total = res[0] + res[1]
    residual = wgtp[...] * jnp.tanh(total * (pair_scale() / saturation) - valp[...])
    for n in range(LEVELS):
        residual = residual + nexts[n] * pltpu.roll(residual, 1 << n, 1)
    over_x = [[[0.0, 0.0] for side in range(2)] for m in range(2)]
    for k in range(8):
        given = residual[k * 16 : k * 16 + 16]
        for above in range(2):
            rows = slice(above * 128 + k * 16, above * 128 + k * 16 + 16)
            for side, lanes in enumerate(HALVES):
                at = first[rows, lanes]
                forcing = jnp.where(at >= 0, take(given, jnp.maximum(at, 0)), 0.0)
                for m in range(2):
                    v = ens[m, rows, lanes].astype(f32) * forcing
                    high, low = split(v)
                    vhi[m, rows, lanes] = high
                    vlo[m, rows, lanes] = low
                    over_x[m][side] = [old + new for old, new in zip(over_x[m][side], line_sums(v, rows))]
    x = summarize(1, over_x)
    share_corners(1)
    complete(1, x)
    share_lines(1)
    for m in range(2):
        field[m] = ctl[m] + local(m)
    @pl.when(core == 0)
    def _():
        arrived(gat, sum_send)
        arrived(gat, back_send)

    @pl.when(core == 1)
    def _():
        arrived(thin.at[pl.ds(0, len(WINDOW))], sum_send)
        arrived(thin, back_send)

    for turn in range(2):
        arrived(corners.at[turn], corner_send.at[turn])
        arrived(lines.at[turn], line_send.at[turn])
    a, b = remote(1)
    side_a[...] = a
    side_b[...] = b


def join(field, side_a, side_b, out, both, sem):
    copies = []
    for quarter in range(4):
        rows = slice(quarter * 64, quarter * 64 + 64)
        update = dot(side_a[:, rows], side_b[...], 0, 0)
        for m in range(2):
            both[m, rows, :] = field[m, rows, :] + update[:, m * TILE : (m + 1) * TILE]
            copy = pltpu.make_async_copy(both.at[m, rows, :], out.at[m, rows, :], sem.at[quarter, m])
            copy.start()
            copies.append(copy)
    for copy in copies:
        copy.wait()


def on_device(control, ensemble, obs_index, obs_value, obs_weight):
    vmem, dma = pltpu.VMEM, pltpu.SemaphoreType.DMA
    square = (TILE, TILE)
    packed = (128, 128)
    field, side_a, side_b = pl.pallas_call(
        kernel,
        out_shape=[vmem((2,) + square, f32), vmem((32, TILE), bf16), vmem((32, 2 * TILE), bf16)],
        in_specs=[pl.BlockSpec(memory_space=pltpu.HBM)] * 5,
        out_specs=[pl.BlockSpec(memory_space=vmem)] * 3,
        scratch_shapes=[
            vmem((2,) + square, f32), vmem((2,) + square, bf16),
            vmem((OBS, TILE), i32), vmem((OBS, TILE), f32), vmem((OBS, TILE), f32),
            vmem(square, bf16), vmem(square, bf16), vmem((2,) + square, bf16), vmem((2,) + square, bf16),
            vmem((2,) + square, f32), vmem(packed, i32), vmem(packed, i32), vmem(square, i32),
            vmem((LEVELS,) + packed, f32), vmem((TILE, 128), f32), vmem((TILE, 128), f32),
            vmem((2, 8, 384), f32), vmem((2, len(LINES), 8, 384), f32), vmem((2, len(CORNERS), 8, 128), f32),
            vmem(packed, f32), vmem((len(COLUMN), WIDE, 128), f32), vmem((len(AROUND), THIN, 128), f32), vmem((WIDE, 128), f32), vmem((2,) + packed, f32),
            vmem(packed, f32), vmem(packed, f32), vmem((TILE, 32), bf16),
            dma((8,)), dma((2,)), dma((2,)), dma((2,)), dma((2,)), dma, dma, dma, dma,
            pltpu.SemaphoreType.REGULAR, pltpu.SemaphoreType.REGULAR, pltpu.SemaphoreType.REGULAR, pltpu.SemaphoreType.REGULAR,
        ],
        compiler_params=pltpu.CompilerParams(
            collective_id=0, has_side_effects=True, vmem_limit_bytes=24 << 20
        ),
    )(*(
        pltpu.with_memory_space_constraint(x, pltpu.HBM)
        for x in (control, ensemble, obs_index.T, obs_value.T, obs_weight.T)
    ))
    return pl.pallas_call(
        join,
        out_shape=jax.ShapeDtypeStruct((2,) + square, f32),
        in_specs=[pl.BlockSpec(memory_space=vmem)] * 3,
        out_specs=pl.BlockSpec(memory_space=pl.ANY),
        scratch_shapes=[vmem((2,) + square, f32), dma((4, 2))],
        compiler_params=pltpu.CompilerParams(vmem_limit_bytes=8 << 20),
    )(field, side_a, side_b)


def solution(mesh):
    return jax.shard_map(
        on_device,
        mesh=mesh,
        in_specs=(
            P("mem", "gx", "gy"),
            P("mem", "gx", "gy"),
            P("gx", "gy"),
            P("gx", "gy"),
            P("gx", "gy"),
        ),
        out_specs=P("mem", "gx", "gy"),
        check_vma=False,
    )
```

```python
import functools
import math

import jax
import jax.numpy as jnp
from jax import lax
from jax.experimental import pallas as pl
from jax.experimental.pallas import tpu as pltpu
from jax.sharding import PartitionSpec as P

LEN = 400
TILE = 256
GRID = 4
RING = 16
NX = GRID * TILE
OBS = 64
saturation = 1.5
MESH = pl.DeviceIdType.MESH
f32 = jnp.float32
bf16 = jnp.bfloat16
i32 = jnp.int32
FAR = 1 << 20

CORNERS = [(dx, dy) for dy in (2, 1, 3) for dx in (2, 3, 1)]
LINES = [(0, 2), (0, 1), (0, 3), (2, 0), (3, 0), (1, 0)]
COLUMN = [8, -7, 7, -6, 6, -5, 5, -4, 4, -3, 3, -2, 2, -1, 1]
AROUND = [(dz, dx) for dz in COLUMN + [0] for dx in (1, 0)][:-1]
WINDOW = [(dz, dx) for dz in (-4, -3, 3, -2, 2, -1, 1, 0) for dx in (1, 0)][:-1]
NEAR = [(-3, 0), (3, 0), (-2, 0), (2, 0), (0, 1), (-1, 0), (1, 0)]
PIECES = 8
WIDE = 16
THIN = 8
LEVELS = 6
HALVES = [slice(0, 128), slice(128, 256)]


def pair_scale():
    decay_rate = math.exp(-1.0 / LEN)
    return (1.0 - decay_rate * decay_rate) / (1.0 + decay_rate * decay_rate)


def decay(steps):
    return jnp.exp(steps.astype(f32) * (-1.0 / LEN))


def split(x):
    high = x.astype(bf16)
    return high, (x - high.astype(f32)).astype(bf16)


def dot(a, b, left=1, right=0):
    return lax.dot_general(a, b, (((left,), (right,)), ((), ())), preferred_element_type=f32)


def take(x, lanes):
    return jnp.take_along_axis(x, lanes, axis=1, mode="promise_in_bounds")


def iota(shape, dim):
    return lax.broadcasted_iota(i32, shape, dim)


def in_plane(dx, dy):
    return {
        "gx": lax.rem(lax.axis_index("gx") + dx, GRID),
        "gy": lax.rem(lax.axis_index("gy") + dy, GRID),
    }


def in_mem(dz, dx):
    mem = lax.axis_index("mem")
    z, half = lax.rem(mem, RING), mem // RING
    return {"mem": lax.rem(half + dx, 2) * RING + lax.rem(z + dz + RING, RING)}


def wide_piece(dz):
    piece = lax.rem(lax.axis_index("mem") + dz + RING, PIECES)
    return pl.ds(pl.multiple_of(piece * WIDE, WIDE), WIDE)


def thin_piece(dz, dx):
    mem = lax.axis_index("mem")
    piece = lax.rem(mem + dz + RING, PIECES) * 2 + lax.rem(mem // RING + dx, 2)
    return pl.ds(pl.multiple_of(piece * THIN, THIN), THIN)


def send(src, dst, send_sem, recv_sem, peer):
    pltpu.make_async_remote_copy(
        src, dst, send_sem, recv_sem, device_id=peer, device_id_type=MESH
    ).start()


def arrived(ref, sem):
    pltpu.make_async_copy(ref, ref, sem).wait()


def coefficients(axis, d, even, shape):
    me = lax.axis_index(axis)
    it = lax.rem(me - d + GRID, GRID)
    before = jnp.where(it < me, TILE * (me - it - 1) + 1, FAR)
    after = jnp.where(it > me, TILE * (it - me - 1) + 1, FAR)
    ends = 2 * NX - TILE * (me + it + 2) + 2
    own = decay(jnp.where(even, before, after))
    above = jnp.where(even, 0.0, -decay(jnp.full(shape, ends, i32)))
    return own, above


def kernel(
    control, ensemble, obs_index, obs_value, obs_weight, field, side_a, side_b,
    ctl, ens, idx, val, wgt, thi, tlo, vhi, vlo, w0, idxp, perm, first, nexts, fcol, bcol,
    msg, lines, corners, pkb, gat, thin, tot, some, res, valp, wgtp, at_ref,
    load_sem, line_send, line_recv, corner_send, corner_recv, sum_send, sum_recv, back_send, back_recv,
    wide_send, wide_recv, near_in, column_in, other_in, all_in, sibling_in,
):
    loads = [
        pltpu.make_async_copy(control.at[m, rows, :], ctl.at[m, rows, :], load_sem.at[2 * m + n])
        for m in range(2)
        for n, rows in enumerate(HALVES)
    ]
    loads += [
        pltpu.make_async_copy(obs_index, idx, load_sem.at[4]),
        pltpu.make_async_copy(ensemble, ens, load_sem.at[5]),
        pltpu.make_async_copy(obs_value, val, load_sem.at[6]),
        pltpu.make_async_copy(obs_weight, wgt, load_sem.at[7]),
    ]
    for copy in loads:
        copy.start()
    barrier = pltpu.get_barrier_semaphore()
    peers = [in_plane(*o) for o in CORNERS] + [in_mem(*o) for o in NEAR] + [in_plane(*o) for o in LINES]

    def signal(sem, peer):
        pl.semaphore_signal(sem, 1, device_id=peer, device_id_type=MESH)

    for peer in peers:
        signal(barrier, peer)
    gx = lax.axis_index("gx")
    core = lax.rem(gx, 2)
    sibling = {"gx": gx + 1 - 2 * core}
    mem = lax.axis_index("mem")
    half, turned = mem // RING, lax.rem(mem, RING) // PIECES

    wide_own, thin_own = wide_piece(0), thin_piece(0, 0)
    square = (TILE, TILE)
    table = decay(jnp.abs(iota(square, 0) - iota(square, 1)))
    high, low = split(table)
    thi[...] = high
    tlo[...] = low
    wide = (8, TILE)
    row, column = iota(wide, 0), iota(wide, 1)
    even = (row & 1) == 0
    ends = decay(jnp.where(even, TILE - 1 - column, column))
    starts = decay(jnp.where(even, column, TILE - 1 - column))
    f_row, b_row = ends[0:1], ends[1:2]
    ends_hi = ends.astype(bf16).astype(f32)
    ends16 = jnp.concatenate([ends_hi, ends - ends_hi], axis=0).astype(bf16)
    narrow = (8, 128)
    lane = iota(narrow, 1)
    left = lane < 64
    cx = [coefficients("gx", d, even, wide) for d in range(GRID)]
    cy = [coefficients("gy", d, even, wide) for d in range(GRID)]
    cl = [coefficients("gy", d, left, narrow) for d in range(GRID)]

    down = iota((TILE, 128), 0)
    fcol[...] = decay(TILE - 1 - down)
    bcol[...] = decay(down)

    def fold(x):
        return x[0:8] + x[8:16]

    def line_sums(v, rows):
        return [jnp.sum((v * col[rows, :]).reshape(-1, 8, 128), axis=0) for col in (fcol, bcol)]

    def summarize(turn, over_x):
        x = 0.0
        for m in range(2):
            for end in range(2):
                line = jnp.concatenate([over_x[m][side][end] for side in range(2)], axis=1)
                x = jnp.where(row == 2 * m + end, jnp.sum(line, axis=0, keepdims=True), x)
        corner_f = jnp.sum(x * f_row, axis=1, keepdims=True)
        corner_b = jnp.sum(x * b_row, axis=1, keepdims=True)
        msg[turn, :, TILE:] = jnp.where(left, corner_f, corner_b)
        return x

    def complete(turn, x):
        for m in range(2):
            y = fold(dot(ends16, vhi[m], 1, 1) + dot(ends16, vlo[m], 1, 1))
            x = jnp.where((row >> 1) == 2 + m, y, x)
        x_hi = x.astype(bf16).astype(f32)
        x16 = jnp.concatenate([x_hi, x - x_hi], axis=0).astype(bf16)
        msg[turn, :, 0:TILE] = fold(dot(x16, thi[...]) + dot(x16, tlo[...]))

    def share_corners(turn):
        for n, o in enumerate(CORNERS):
            send(
                msg.at[turn, :, pl.ds(TILE, 128)], corners.at[turn, n],
                corner_send.at[turn], corner_recv.at[turn], in_plane(*o),
            )

    def share_lines(turn):
        for n, o in enumerate(LINES):
            send(msg.at[turn], lines.at[turn, n], line_send.at[turn], line_recv.at[turn], in_plane(*o))

    def local(m):
        u = dot(thi[...], vhi[m]) + dot(tlo[...], vhi[m]) + dot(thi[...], vlo[m])
        uhi, ulo = split(u)
        return dot(uhi, thi[...]) + dot(ulo, thi[...]) + dot(uhi, tlo[...])

    def remote(turn):
        arrived(corners.at[turn], corner_recv.at[turn])
        arrived(lines.at[turn], line_recv.at[turn])

        def block(dx, dy):
            if (dx, dy) == (0, 0):
                return msg[turn]
            return lines[turn, LINES.index((dx, dy))]

        def weigh(c, x):
            return c[0] * x + c[1] * pltpu.roll(x, 1, 0)

        xs, ys, corner = 0.0, 0.0, 0.0
        for d in range(GRID):
            xs = xs + weigh(cx[d], block(d, 0)[:, 0:TILE])
            ys = ys + weigh(cy[d], block(0, d)[:, 0:TILE])
        for dy in range(GRID):
            over_x = 0.0
            for dx in range(GRID):
                if dx and dy:
                    g = corners[turn, CORNERS.index((dx, dy))]
                else:
                    g = block(dx, dy)[:, TILE:]
                over_x = over_x + weigh((cx[dx][0][:, 0:128], cx[dx][1][:, 0:128]), g)
            corner = corner + cl[dy][0] * over_x + cl[dy][1] * pltpu.roll(over_x, 64, 1)
        ab = jnp.where(row < 4, xs + corner[:, 0:1] * b_row + corner[:, 64:65] * f_row, ys)
        a = jnp.where(row < 4, starts, ab)
        b = jnp.where(row < 4, ab, starts)
        b = jnp.concatenate([jnp.where((row & 2) == 0, b, 0.0), jnp.where((row & 2) == 0, 0.0, b)], axis=1)
        a_hi, b_hi = a.astype(bf16).astype(f32), b.astype(bf16).astype(f32)
        a_lo, b_lo = a - a_hi, b - b_hi
        a = jnp.concatenate([a_hi, a_hi, a_lo, a_lo], axis=0).astype(bf16)
        b = jnp.concatenate([b_hi, b_lo, b_hi, b_lo], axis=0).astype(bf16)
        return a, b

    def pack(ref):
        return jnp.concatenate([ref[:, 0:128], ref[:, 128:256]], axis=0).T

    over_x = [[[0.0, 0.0] for side in range(2)] for m in range(2)]

    def add_sums(m, side, v, rows):
        over_x[m][side] = [old + new for old, new in zip(over_x[m][side], line_sums(v, rows))]

    for m in range(2):
        for n, rows in enumerate(HALVES):
            loads[2 * m + n].wait()
            high, low = split(ctl[m, rows, :])
            vhi[m, rows, :] = high
            vlo[m, rows, :] = low
            for side, lanes in enumerate(HALVES):
                add_sums(m, side, ctl[m, rows, lanes], rows)
    complete(0, summarize(0, over_x))
    pl.semaphore_wait(barrier, len(peers))
    for dz in (-3, 3):
        signal(near_in, in_mem(dz, 0))
    share_corners(0)
    share_lines(0)
    for m in range(2):
        w0[m] = local(m)
    loads[4].wait()
    level = iota(narrow, 0)
    order = []
    for side in range(2):
        at = [idx[8 * t : 8 * t + 8, side * 128 : side * 128 + 128] for t in range(8)]
        rank = [jnp.zeros(narrow, i32) for t in range(8)]
        for j in range(OBS):
            here = at[j // 8][j % 8 : j % 8 + 1]
            for t in range(8):
                if t < j // 8:
                    ahead = here < at[t]
                elif t > j // 8:
                    ahead = here <= at[t]
                else:
                    ahead = (here < at[t]) | ((here == at[t]) & (level > j % 8))
                rank[t] = rank[t] + jnp.where(ahead, 1, 0)
        found = [jnp.zeros(narrow, i32) for t in range(8)]
        for j in range(OBS):
            place_of = rank[j // 8][j % 8 : j % 8 + 1]
            for t in range(8):
                found[t] = jnp.where(place_of == level + 8 * t, side * OBS + j, found[t])
        order += found
    perm[...] = jnp.concatenate(order, axis=0).T
    idxp[...] = take(pack(idx), perm[...])
    loads[5].wait()
    pl.semaphore_wait(near_in, 2)
    for dz in (-2, 2):
        signal(column_in, in_mem(dz, 0))
    signal(other_in, in_mem(0, 1))
    a, b = remote(0)
    at_ref[...] = a.T
    for k in range(4):
        fields = []
        for above in range(2):
            rows = slice(above * 128 + k * 32, above * 128 + k * 32 + 32)
            update = dot(at_ref[rows, :], b)
            fields.append(
                ens[0, rows, :].astype(f32) * (w0[0, rows, :] + update[:, 0:TILE])
                + ens[1, rows, :].astype(f32) * (w0[1, rows, :] + update[:, TILE:])
            )
        for n in range(0, 32, 8):
            rows = slice(n, n + 8)
            at = idxp[k * 32 + n : k * 32 + n + 8, :]
            low = at & 127
            upper = at >= 128
            picked = [jnp.where(upper, take(v[rows, 128:256], low), take(v[rows, 0:128], low)) for v in fields]
            pkb[k * 32 + n : k * 32 + n + 8, :] = jnp.where(left, *picked)

    pl.semaphore_wait(column_in, 2)
    pl.semaphore_wait(other_in, 1)
    signal(all_in, in_mem(0, 1))
    signal(sibling_in, sibling)

    @pl.when(core == 0)
    def _():
        pl.semaphore_wait(sibling_in, 1)
        for n, dz in enumerate(COLUMN + [0]):
            send(pkb.at[wide_piece(dz)], gat.at[n], sum_send, wide_recv, in_mem(dz, 0) | sibling)

    @pl.when(core == 1)
    def _():
        for n, o in enumerate(WINDOW):
            send(pkb.at[thin_piece(*o)], thin.at[n], sum_send, sum_recv, in_mem(*o))

    cells = idxp[...].T
    for side in range(2):
        idx[:, side * 128 : side * 128 + 128] = cells[side * OBS : side * OBS + OBS]

    def find(k, carry):
        rows = pl.ds(pl.multiple_of((k // 2) * 128, 128), 128)
        lanes = pl.ds(pl.multiple_of((k % 2) * 128, 128), 128)
        cell = iota((128, 128), 0) + (k % 2) * 128
        found = jnp.full((128, 128), -1, i32)
        for j in range(OBS):
            found = jnp.where(idx[j : j + 1, rows] == cell, (k // 2) * OBS + j, found)
        first[rows, lanes] = found.T
        return carry

    lax.fori_loop(0, 4, find, 0)
    cells = idxp[...] + jnp.where(iota((128, 128), 1) < OBS, 0, TILE)
    for n in range(LEVELS):
        nexts[n] = jnp.where(cells == pltpu.roll(cells, 1 << n, 1), 1.0, 0.0)
    loads[6].wait()
    loads[7].wait()
    valp[...] = take(pack(val), perm[...]) * (1.0 / saturation)
    wgtp[...] = take(pack(wgt), perm[...]) * (saturation * pair_scale())
    pl.semaphore_wait(all_in, 1)

    @pl.when(core == 1)
    def _():
        arrived(thin.at[pl.ds(0, len(WINDOW))], sum_recv)
        some[...] = pkb[thin_own, :] + jnp.sum(thin[0 : len(WINDOW)], axis=0)
        for o in AROUND:
            send(some, res.at[turned, thin_own], back_send, back_recv, in_mem(*o))
        res[turned, thin_own, :] = some[...]
        pl.semaphore_wait(sibling_in, 1)
        arrived(gat, wide_recv)
        tot[...] = jnp.sum(gat[...], axis=0)
        for o in WINDOW + [(0, 0)]:
            send(tot, res.at[half, wide_own], wide_send, back_recv, in_mem(*o) | sibling)
        arrived(thin, back_recv)

    @pl.when(core == 0)
    def _():
        arrived(res, back_recv)

    total = res[0] + res[1]
    residual = wgtp[...] * jnp.tanh(total * (pair_scale() / saturation) - valp[...])
    for n in range(LEVELS):
        residual = residual + nexts[n] * pltpu.roll(residual, 1 << n, 1)
    over_x = [[[0.0, 0.0] for side in range(2)] for m in range(2)]
    for k in range(8):
        given = residual[k * 16 : k * 16 + 16]
        for above in range(2):
            rows = slice(above * 128 + k * 16, above * 128 + k * 16 + 16)
            for side, lanes in enumerate(HALVES):
                at = first[rows, lanes]
                forcing = jnp.where(at >= 0, take(given, jnp.maximum(at, 0)), 0.0)
                for m in range(2):
                    v = ens[m, rows, lanes].astype(f32) * forcing
                    high, low = split(v)
                    vhi[m, rows, lanes] = high
                    vlo[m, rows, lanes] = low
                    over_x[m][side] = [old + new for old, new in zip(over_x[m][side], line_sums(v, rows))]
    x = summarize(1, over_x)
    share_corners(1)
    complete(1, x)
    share_lines(1)
    for m in range(2):
        field[m] = ctl[m] + local(m)
    @pl.when(core == 0)
    def _():
        arrived(gat, sum_send)

    @pl.when(core == 1)
    def _():
        arrived(thin.at[pl.ds(0, len(WINDOW))], sum_send)
        arrived(thin, back_send)
        arrived(gat, wide_send)

    for turn in range(2):
        arrived(corners.at[turn], corner_send.at[turn])
        arrived(lines.at[turn], line_send.at[turn])
    a, b = remote(1)
    side_a[...] = a
    side_b[...] = b


def join(field, side_a, side_b, out, both, sem):
    copies = []
    for quarter in range(4):
        rows = slice(quarter * 64, quarter * 64 + 64)
        update = dot(side_a[:, rows], side_b[...], 0, 0)
        for m in range(2):
            both[m, rows, :] = field[m, rows, :] + update[:, m * TILE : (m + 1) * TILE]
            copy = pltpu.make_async_copy(both.at[m, rows, :], out.at[m, rows, :], sem.at[quarter, m])
            copy.start()
            copies.append(copy)
    for copy in copies:
        copy.wait()


def on_device(control, ensemble, obs_index, obs_value, obs_weight):
    vmem, dma = pltpu.VMEM, pltpu.SemaphoreType.DMA
    square = (TILE, TILE)
    packed = (128, 128)
    field, side_a, side_b = pl.pallas_call(
        kernel,
        out_shape=[vmem((2,) + square, f32), vmem((32, TILE), bf16), vmem((32, 2 * TILE), bf16)],
        in_specs=[pl.BlockSpec(memory_space=pltpu.HBM)] * 5,
        out_specs=[pl.BlockSpec(memory_space=vmem)] * 3,
        scratch_shapes=[
            vmem((2,) + square, f32), vmem((2,) + square, bf16),
            vmem((OBS, TILE), i32), vmem((OBS, TILE), f32), vmem((OBS, TILE), f32),
            vmem(square, bf16), vmem(square, bf16), vmem((2,) + square, bf16), vmem((2,) + square, bf16),
            vmem((2,) + square, f32), vmem(packed, i32), vmem(packed, i32), vmem(square, i32),
            vmem((LEVELS,) + packed, f32), vmem((TILE, 128), f32), vmem((TILE, 128), f32),
            vmem((2, 8, 384), f32), vmem((2, len(LINES), 8, 384), f32), vmem((2, len(CORNERS), 8, 128), f32),
            vmem(packed, f32), vmem((RING, WIDE, 128), f32), vmem((len(AROUND), THIN, 128), f32), vmem((WIDE, 128), f32), vmem((THIN, 128), f32), vmem((2,) + packed, f32),
            vmem(packed, f32), vmem(packed, f32), vmem((TILE, 32), bf16),
            dma((8,)), dma((2,)), dma((2,)), dma((2,)), dma((2,)), dma, dma, dma, dma, dma, dma,
            pltpu.SemaphoreType.REGULAR, pltpu.SemaphoreType.REGULAR, pltpu.SemaphoreType.REGULAR, pltpu.SemaphoreType.REGULAR, pltpu.SemaphoreType.REGULAR,
        ],
        compiler_params=pltpu.CompilerParams(
            collective_id=0, has_side_effects=True, vmem_limit_bytes=24 << 20
        ),
    )(*(
        pltpu.with_memory_space_constraint(x, pltpu.HBM)
        for x in (control, ensemble, obs_index.T, obs_value.T, obs_weight.T)
    ))
    return pl.pallas_call(
        join,
        out_shape=jax.ShapeDtypeStruct((2,) + square, f32),
        in_specs=[pl.BlockSpec(memory_space=vmem)] * 3,
        out_specs=pl.BlockSpec(memory_space=pl.ANY),
        scratch_shapes=[vmem((2,) + square, f32), dma((4, 2))],
        compiler_params=pltpu.CompilerParams(vmem_limit_bytes=8 << 20),
    )(field, side_a, side_b)


def solution(mesh):
    return jax.shard_map(
        on_device,
        mesh=mesh,
        in_specs=(
            P("mem", "gx", "gy"),
            P("mem", "gx", "gy"),
            P("gx", "gy"),
            P("gx", "gy"),
            P("gx", "gy"),
        ),
        out_specs=P("mem", "gx", "gy"),
        check_vma=False,
    )
```

```python
import functools
import math

import jax
import jax.numpy as jnp
from jax import lax
from jax.experimental import pallas as pl
from jax.experimental.pallas import tpu as pltpu
from jax.sharding import PartitionSpec as P

LEN = 400
TILE = 256
GRID = 4
RING = 16
NX = GRID * TILE
OBS = 64
saturation = 1.5
MESH = pl.DeviceIdType.MESH
f32 = jnp.float32
bf16 = jnp.bfloat16
i32 = jnp.int32
FAR = 1 << 20

CORNERS = [(dx, dy) for dy in (2, 1, 3) for dx in (2, 3, 1)]
LINES = [(0, 2), (0, 1), (0, 3), (2, 0), (3, 0), (1, 0)]
COLUMN = [8, -7, 7, -6, 6, -5, 5, -4, 4, -3, 3, -2, 2, -1, 1]
AROUND = [(dz, dx) for dz in COLUMN + [0] for dx in (1, 0)][:-1]
WINDOW = [(dz, dx) for dz in (-4, -3, 3, -2, 2, -1, 1, 0) for dx in (1, 0)][:-1]
NEAR = [(-3, 0), (3, 0), (-2, 0), (2, 0), (0, 1), (-1, 0), (1, 0)]
PIECES = 8
WIDE = 16
THIN = 8
LEVELS = 6
HALVES = [slice(0, 128), slice(128, 256)]


def pair_scale():
    decay_rate = math.exp(-1.0 / LEN)
    return (1.0 - decay_rate * decay_rate) / (1.0 + decay_rate * decay_rate)


def decay(steps):
    return jnp.exp(steps.astype(f32) * (-1.0 / LEN))


def split(x):
    high = x.astype(bf16)
    return high, (x - high.astype(f32)).astype(bf16)


def dot(a, b, left=1, right=0):
    return lax.dot_general(a, b, (((left,), (right,)), ((), ())), preferred_element_type=f32)


def take(x, lanes):
    return jnp.take_along_axis(x, lanes, axis=1, mode="promise_in_bounds")


def iota(shape, dim):
    return lax.broadcasted_iota(i32, shape, dim)


def in_plane(dx, dy):
    return {
        "gx": lax.rem(lax.axis_index("gx") + dx, GRID),
        "gy": lax.rem(lax.axis_index("gy") + dy, GRID),
    }


def in_mem(dz, dx):
    mem = lax.axis_index("mem")
    z, half = lax.rem(mem, RING), mem // RING
    return {"mem": lax.rem(half + dx, 2) * RING + lax.rem(z + dz + RING, RING)}


def wide_piece(dz):
    piece = lax.rem(lax.axis_index("mem") + dz + RING, PIECES)
    return pl.ds(pl.multiple_of(piece * WIDE, WIDE), WIDE)


def thin_piece(dz, dx):
    mem = lax.axis_index("mem")
    piece = lax.rem(mem + dz + RING, PIECES) * 2 + lax.rem(mem // RING + dx, 2)
    return pl.ds(pl.multiple_of(piece * THIN, THIN), THIN)


def send(src, dst, send_sem, recv_sem, peer):
    pltpu.make_async_remote_copy(
        src, dst, send_sem, recv_sem, device_id=peer, device_id_type=MESH
    ).start()


def arrived(ref, sem):
    pltpu.make_async_copy(ref, ref, sem).wait()


def coefficients(axis, d, even, shape):
    me = lax.axis_index(axis)
    it = lax.rem(me - d + GRID, GRID)
    before = jnp.where(it < me, TILE * (me - it - 1) + 1, FAR)
    after = jnp.where(it > me, TILE * (it - me - 1) + 1, FAR)
    ends = 2 * NX - TILE * (me + it + 2) + 2
    own = decay(jnp.where(even, before, after))
    above = jnp.where(even, 0.0, -decay(jnp.full(shape, ends, i32)))
    return own, above


def kernel(
    control, ensemble, obs_index, obs_value, obs_weight, field, side_a, side_b,
    ctl, ens, idx, val, wgt, thi, tlo, vhi, vlo, w0, idxp, perm, first, nexts, fcol, bcol,
    msg, lines, corners, pkb, gat, thin, tot, some, res, valp, wgtp, at_ref,
    load_sem, line_send, line_recv, corner_send, corner_recv, sum_send, sum_recv, back_send, back_recv,
    wide_send, wide_recv, near_in, column_in, other_in, all_in, sibling_in,
):
    loads = [
        pltpu.make_async_copy(control.at[m, rows, :], ctl.at[m, rows, :], load_sem.at[2 * m + n])
        for m in range(2)
        for n, rows in enumerate(HALVES)
    ]
    loads += [
        pltpu.make_async_copy(obs_index, idx, load_sem.at[4]),
        pltpu.make_async_copy(ensemble, ens, load_sem.at[5]),
        pltpu.make_async_copy(obs_value, val, load_sem.at[6]),
        pltpu.make_async_copy(obs_weight, wgt, load_sem.at[7]),
    ]
    for copy in loads:
        copy.start()
    barrier = pltpu.get_barrier_semaphore()
    peers = [in_plane(*o) for o in CORNERS] + [in_mem(*o) for o in NEAR] + [in_plane(*o) for o in LINES]

    def signal(sem, peer):
        pl.semaphore_signal(sem, 1, device_id=peer, device_id_type=MESH)

    for peer in peers:
        signal(barrier, peer)
    gx = lax.axis_index("gx")
    core = lax.rem(gx, 2)
    sibling = {"gx": gx + 1 - 2 * core}
    mem = lax.axis_index("mem")
    half, turned = mem // RING, lax.rem(mem, RING) // PIECES

    wide_own, thin_own = wide_piece(0), thin_piece(0, 0)
    square = (TILE, TILE)
    table = decay(jnp.abs(iota(square, 0) - iota(square, 1)))
    high, low = split(table)
    thi[...] = high
    tlo[...] = low
    wide = (8, TILE)
    row, column = iota(wide, 0), iota(wide, 1)
    even = (row & 1) == 0
    ends = decay(jnp.where(even, TILE - 1 - column, column))
    starts = decay(jnp.where(even, column, TILE - 1 - column))
    f_row, b_row = ends[0:1], ends[1:2]
    ends_hi = ends.astype(bf16).astype(f32)
    ends16 = jnp.concatenate([ends_hi, ends - ends_hi], axis=0).astype(bf16)
    narrow = (8, 128)
    lane = iota(narrow, 1)
    left = lane < 64
    cx = [coefficients("gx", d, even, wide) for d in range(GRID)]
    cy = [coefficients("gy", d, even, wide) for d in range(GRID)]
    cl = [coefficients("gy", d, left, narrow) for d in range(GRID)]

    down = iota((TILE, 128), 0)
    fcol[...] = decay(TILE - 1 - down)
    bcol[...] = decay(down)

    def fold(x):
        return x[0:8] + x[8:16]

    def line_sums(v, rows):
        return [jnp.sum((v * col[rows, :]).reshape(-1, 8, 128), axis=0) for col in (fcol, bcol)]

    def summarize(turn, over_x):
        x = 0.0
        for m in range(2):
            for end in range(2):
                line = jnp.concatenate([over_x[m][side][end] for side in range(2)], axis=1)
                x = jnp.where(row == 2 * m + end, jnp.sum(line, axis=0, keepdims=True), x)
        corner_f = jnp.sum(x * f_row, axis=1, keepdims=True)
        corner_b = jnp.sum(x * b_row, axis=1, keepdims=True)
        msg[turn, :, TILE:] = jnp.where(left, corner_f, corner_b)
        return x

    def complete(turn, x):
        for m in range(2):
            y = fold(dot(ends16, vhi[m], 1, 1) + dot(ends16, vlo[m], 1, 1))
            x = jnp.where((row >> 1) == 2 + m, y, x)
        x_hi = x.astype(bf16).astype(f32)
        x16 = jnp.concatenate([x_hi, x - x_hi], axis=0).astype(bf16)
        msg[turn, :, 0:TILE] = fold(dot(x16, thi[...]) + dot(x16, tlo[...]))

    def share_corners(turn):
        for n, o in enumerate(CORNERS):
            send(
                msg.at[turn, :, pl.ds(TILE, 128)], corners.at[turn, n],
                corner_send.at[turn], corner_recv.at[turn], in_plane(*o),
            )

    def share_lines(turn):
        for n, o in enumerate(LINES):
            send(msg.at[turn], lines.at[turn, n], line_send.at[turn], line_recv.at[turn], in_plane(*o))

    def local(m):
        u = dot(thi[...], vhi[m]) + dot(tlo[...], vhi[m]) + dot(thi[...], vlo[m])
        uhi, ulo = split(u)
        return dot(uhi, thi[...]) + dot(ulo, thi[...]) + dot(uhi, tlo[...])

    def remote(turn):
        arrived(corners.at[turn], corner_recv.at[turn])
        arrived(lines.at[turn], line_recv.at[turn])

        def block(dx, dy):
            if (dx, dy) == (0, 0):
                return msg[turn]
            return lines[turn, LINES.index((dx, dy))]

        def weigh(c, x):
            return c[0] * x + c[1] * pltpu.roll(x, 1, 0)

        xs, ys, corner = 0.0, 0.0, 0.0
        for d in range(GRID):
            xs = xs + weigh(cx[d], block(d, 0)[:, 0:TILE])
            ys = ys + weigh(cy[d], block(0, d)[:, 0:TILE])
        for dy in range(GRID):
            over_x = 0.0
            for dx in range(GRID):
                if dx and dy:
                    g = corners[turn, CORNERS.index((dx, dy))]
                else:
                    g = block(dx, dy)[:, TILE:]
                over_x = over_x + weigh((cx[dx][0][:, 0:128], cx[dx][1][:, 0:128]), g)
            corner = corner + cl[dy][0] * over_x + cl[dy][1] * pltpu.roll(over_x, 64, 1)
        ab = jnp.where(row < 4, xs + corner[:, 0:1] * b_row + corner[:, 64:65] * f_row, ys)
        a = jnp.where(row < 4, starts, ab)
        b = jnp.where(row < 4, ab, starts)
        b = jnp.concatenate([jnp.where((row & 2) == 0, b, 0.0), jnp.where((row & 2) == 0, 0.0, b)], axis=1)
        a_hi, b_hi = a.astype(bf16).astype(f32), b.astype(bf16).astype(f32)
        a_lo, b_lo = a - a_hi, b - b_hi
        a = jnp.concatenate([a_hi, a_hi, a_lo, a_lo], axis=0).astype(bf16)
        b = jnp.concatenate([b_hi, b_lo, b_hi, b_lo], axis=0).astype(bf16)
        return a, b

    def pack(ref):
        return jnp.concatenate([ref[:, 0:128], ref[:, 128:256]], axis=0).T

    over_x = [[[0.0, 0.0] for side in range(2)] for m in range(2)]

    def add_sums(m, side, v, rows):
        over_x[m][side] = [old + new for old, new in zip(over_x[m][side], line_sums(v, rows))]

    for m in range(2):
        for n, rows in enumerate(HALVES):
            loads[2 * m + n].wait()
            high, low = split(ctl[m, rows, :])
            vhi[m, rows, :] = high
            vlo[m, rows, :] = low
            for side, lanes in enumerate(HALVES):
                add_sums(m, side, ctl[m, rows, lanes], rows)
    complete(0, summarize(0, over_x))
    pl.semaphore_wait(barrier, len(peers))
    for dz in (-3, 3):
        signal(near_in, in_mem(dz, 0))
    share_corners(0)
    share_lines(0)
    for m in range(2):
        w0[m] = local(m)
    loads[4].wait()
    level = iota(narrow, 0)
    order = []
    for side in range(2):
        at = [idx[8 * t : 8 * t + 8, side * 128 : side * 128 + 128] for t in range(8)]
        rank = [jnp.zeros(narrow, i32) for t in range(8)]
        for j in range(OBS):
            here = at[j // 8][j % 8 : j % 8 + 1]
            for t in range(8):
                if t < j // 8:
                    ahead = here < at[t]
                elif t > j // 8:
                    ahead = here <= at[t]
                else:
                    ahead = (here < at[t]) | ((here == at[t]) & (level > j % 8))
                rank[t] = rank[t] + jnp.where(ahead, 1, 0)
        found = [jnp.zeros(narrow, i32) for t in range(8)]
        for j in range(OBS):
            place_of = rank[j // 8][j % 8 : j % 8 + 1]
            for t in range(8):
                found[t] = jnp.where(place_of == level + 8 * t, side * OBS + j, found[t])
        order += found
    perm[...] = jnp.concatenate(order, axis=0).T
    idxp[...] = take(pack(idx), perm[...])
    loads[5].wait()
    pl.semaphore_wait(near_in, 2)
    for dz in (-2, 2):
        signal(column_in, in_mem(dz, 0))
    signal(other_in, in_mem(0, 1))
    a, b = remote(0)
    at_ref[...] = a.T
    for k in range(4):
        fields = []
        for above in range(2):
            rows = slice(above * 128 + k * 32, above * 128 + k * 32 + 32)
            update = dot(at_ref[rows, :], b)
            fields.append(
                ens[0, rows, :].astype(f32) * (w0[0, rows, :] + update[:, 0:TILE])
                + ens[1, rows, :].astype(f32) * (w0[1, rows, :] + update[:, TILE:])
            )
        for n in range(0, 32, 8):
            rows = slice(n, n + 8)
            at = idxp[k * 32 + n : k * 32 + n + 8, :]
            low = at & 127
            upper = at >= 128
            picked = [jnp.where(upper, take(v[rows, 128:256], low), take(v[rows, 0:128], low)) for v in fields]
            pkb[k * 32 + n : k * 32 + n + 8, :] = jnp.where(left, *picked)

    pl.semaphore_wait(column_in, 2)
    pl.semaphore_wait(other_in, 1)
    signal(all_in, in_mem(0, 1))
    signal(sibling_in, sibling)

    @pl.when(core == 0)
    def _():
        pl.semaphore_wait(sibling_in, 1)
        for n, dz in enumerate(COLUMN + [0]):
            send(pkb.at[wide_piece(dz)], gat.at[n], sum_send, wide_recv, in_mem(dz, 0) | sibling)

    @pl.when(core == 1)
    def _():
        for n, o in enumerate(WINDOW):
            send(pkb.at[thin_piece(*o)], thin.at[n], sum_send, sum_recv, in_mem(*o))

    cells = idxp[...].T
    for side in range(2):
        idx[:, side * 128 : side * 128 + 128] = cells[side * OBS : side * OBS + OBS]

    def find(k, carry):
        rows = pl.ds(pl.multiple_of((k // 2) * 128, 128), 128)
        lanes = pl.ds(pl.multiple_of((k % 2) * 128, 128), 128)
        cell = iota((128, 128), 0) + (k % 2) * 128
        found = jnp.full((128, 128), -1, i32)
        for j in range(OBS):
            found = jnp.where(idx[j : j + 1, rows] == cell, (k // 2) * OBS + j, found)
        first[rows, lanes] = found.T
        return carry

    lax.fori_loop(0, 4, find, 0)
    cells = idxp[...] + jnp.where(iota((128, 128), 1) < OBS, 0, TILE)
    for n in range(LEVELS):
        nexts[n] = jnp.where(cells == pltpu.roll(cells, 1 << n, 1), 1.0, 0.0)
    loads[6].wait()
    loads[7].wait()
    valp[...] = take(pack(val), perm[...]) * (1.0 / saturation)
    wgtp[...] = take(pack(wgt), perm[...]) * (saturation * pair_scale())
    pl.semaphore_wait(all_in, 1)

    @pl.when(core == 1)
    def _():
        arrived(thin.at[pl.ds(0, len(WINDOW))], sum_recv)
        some[...] = pkb[thin_own, :] + jnp.sum(thin[0 : len(WINDOW)], axis=0)
        for o in AROUND:
            send(some, res.at[turned, thin_own], back_send, back_recv, in_mem(*o))
        res[turned, thin_own, :] = some[...]
        pl.semaphore_wait(sibling_in, 1)
        arrived(gat, wide_recv)
        tot[...] = jnp.sum(gat[...], axis=0)
        for o in WINDOW + [(0, 0)]:
            send(tot, res.at[half, wide_own], wide_send, back_recv, in_mem(*o) | sibling)
        arrived(thin, back_recv)

    @pl.when(core == 0)
    def _():
        arrived(res, back_recv)

    total = res[0] + res[1]
    residual = wgtp[...] * jnp.tanh(total * (pair_scale() / saturation) - valp[...])
    for n in range(LEVELS):
        residual = residual + nexts[n] * pltpu.roll(residual, 1 << n, 1)
    over_x = [[[0.0, 0.0] for side in range(2)] for m in range(2)]
    for k in range(8):
        given = residual[k * 16 : k * 16 + 16]
        for above in range(2):
            rows = slice(above * 128 + k * 16, above * 128 + k * 16 + 16)
            for side, lanes in enumerate(HALVES):
                at = first[rows, lanes]
                forcing = jnp.where(at >= 0, take(given, jnp.maximum(at, 0)), 0.0)
                for m in range(2):
                    v = ens[m, rows, lanes].astype(f32) * forcing
                    high, low = split(v)
                    vhi[m, rows, lanes] = high
                    vlo[m, rows, lanes] = low
                    over_x[m][side] = [old + new for old, new in zip(over_x[m][side], line_sums(v, rows))]
    x = summarize(1, over_x)
    share_corners(1)
    complete(1, x)
    share_lines(1)
    for m in range(2):
        field[m] = ctl[m] + local(m)
    @pl.when(core == 0)
    def _():
        arrived(gat, sum_send)

    @pl.when(core == 1)
    def _():
        arrived(thin.at[pl.ds(0, len(WINDOW))], sum_send)
        arrived(thin, back_send)
        arrived(gat, wide_send)

    for turn in range(2):
        arrived(corners.at[turn], corner_send.at[turn])
        arrived(lines.at[turn], line_send.at[turn])
    a, b = remote(1)
    side_a[...] = a.T
    side_b[...] = b


def join(field, side_a, side_b, out, both, sem):
    copies = []
    for quarter in range(4):
        rows = slice(quarter * 64, quarter * 64 + 64)
        update = dot(side_a[rows, :], side_b[...])
        for m in range(2):
            both[m, rows, :] = field[m, rows, :] + update[:, m * TILE : (m + 1) * TILE]
            copy = pltpu.make_async_copy(both.at[m, rows, :], out.at[m, rows, :], sem.at[quarter, m])
            copy.start()
            copies.append(copy)
    for copy in copies:
        copy.wait()


def on_device(control, ensemble, obs_index, obs_value, obs_weight):
    vmem, dma = pltpu.VMEM, pltpu.SemaphoreType.DMA
    square = (TILE, TILE)
    packed = (128, 128)
    field, side_a, side_b = pl.pallas_call(
        kernel,
        out_shape=[vmem((2,) + square, f32), vmem((TILE, 32), bf16), vmem((32, 2 * TILE), bf16)],
        in_specs=[pl.BlockSpec(memory_space=pltpu.HBM)] * 5,
        out_specs=[pl.BlockSpec(memory_space=vmem)] * 3,
        scratch_shapes=[
            vmem((2,) + square, f32), vmem((2,) + square, bf16),
            vmem((OBS, TILE), i32), vmem((OBS, TILE), f32), vmem((OBS, TILE), f32),
            vmem(square, bf16), vmem(square, bf16), vmem((2,) + square, bf16), vmem((2,) + square, bf16),
            vmem((2,) + square, f32), vmem(packed, i32), vmem(packed, i32), vmem(square, i32),
            vmem((LEVELS,) + packed, f32), vmem((TILE, 128), f32), vmem((TILE, 128), f32),
            vmem((2, 8, 384), f32), vmem((2, len(LINES), 8, 384), f32), vmem((2, len(CORNERS), 8, 128), f32),
            vmem(packed, f32), vmem((RING, WIDE, 128), f32), vmem((len(AROUND), THIN, 128), f32), vmem((WIDE, 128), f32), vmem((THIN, 128), f32), vmem((2,) + packed, f32),
            vmem(packed, f32), vmem(packed, f32), vmem((TILE, 32), bf16),
            dma((8,)), dma((2,)), dma((2,)), dma((2,)), dma((2,)), dma, dma, dma, dma, dma, dma,
            pltpu.SemaphoreType.REGULAR, pltpu.SemaphoreType.REGULAR, pltpu.SemaphoreType.REGULAR, pltpu.SemaphoreType.REGULAR, pltpu.SemaphoreType.REGULAR,
        ],
        compiler_params=pltpu.CompilerParams(
            collective_id=0, has_side_effects=True, vmem_limit_bytes=24 << 20
        ),
    )(*(
        pltpu.with_memory_space_constraint(x, pltpu.HBM)
        for x in (control, ensemble, obs_index.T, obs_value.T, obs_weight.T)
    ))
    return pl.pallas_call(
        join,
        out_shape=jax.ShapeDtypeStruct((2,) + square, f32),
        in_specs=[pl.BlockSpec(memory_space=vmem)] * 3,
        out_specs=pl.BlockSpec(memory_space=pl.ANY),
        scratch_shapes=[vmem((2,) + square, f32), dma((4, 2))],
        compiler_params=pltpu.CompilerParams(vmem_limit_bytes=8 << 20),
    )(field, side_a, side_b)


def solution(mesh):
    return jax.shard_map(
        on_device,
        mesh=mesh,
        in_specs=(
            P("mem", "gx", "gy"),
            P("mem", "gx", "gy"),
            P("gx", "gy"),
            P("gx", "gy"),
            P("gx", "gy"),
        ),
        out_specs=P("mem", "gx", "gy"),
        check_vma=False,
    )
```
